32 devices in a mesh: tok: 32 (over z, y, x, core), head: 1.
Axes of the slice: x: 2, y: 2, z: 4, core: 2. Of those that a mesh axis runs over, the one named last changes fastest.
Arguments:
- tokens: bfloat16 [8192, 2048], P('tok', 'head'), may hold values from -6 to 6
- norm_gain: float32 [2048], replicated, may hold values from 0.25 to 1.75
- w_query: bfloat16 [2048, 4096], P('tok', 'head'), may hold values from -0.125 to 0.125
- key_weight: bfloat16 [2048, 512], P('tok', 'head'), may hold values from -0.125 to 0.125
- value_weight: bfloat16 [2048, 512], P('tok', 'head'), may hold values from -0.125 to 0.125
- query_gain: float32 [128], replicated, may hold values from 0.6 to 12
- key_gain: float32 [128], replicated, may hold values from 0.6 to 12
- w_out: bfloat16 [4096, 2048], P('head', 'tok'), may hold values from -0.09375 to 0.09375
- doc_ids: int32 [8192], P('tok'), may hold values from 0 to 3, never falling along the last dimension, each value on 1 to 4096 neighbouring positions
- sentinel: int32 [8192], P('tok'), may hold values 0 or 1
- tile_reach: int32 [64], P('tok'), may hold values from 1 to 28, as said below
Outputs:
- attn_out: bfloat16 [8192, 2048], P('tok', 'head')
The draws below stay inside these ranges and needn't reach their ends.
Inputs may be any that keep to these rules, and one draw needn't show every extreme that they name: `tile_reach`: some tile's entry is 28.
All inputs are finite; a program needn't handle non-finite values. No bound on the sum of `sentinel` on one device may be relied on, other than what follows from the above.
Results may differ from the reference program's by a relative error of at most 0.014.
The reference program's roundings to bfloat16 on the way count: a program that leaves them out, or rounds other values in their place, can miss the bound.
Values may be sent and summed in bfloat16 or wider, within the bound.
A program may use at most 128 MiB of HBM per device.

```python
import math
import jax
import jax.numpy as jnp
import numpy as np
from jax import lax

MODEL_WIDTH = 2048
QUERY_HEADS = 32
KEY_VALUE_HEADS = 4
HEAD_SIZE = 128
TILE_TOKENS = 128
SPAN_TILES = 28
STREAM_TOKENS = 8192
QTILES = 64
DOCS = 4
DOC_MOST = 4096
N_HEAD = 1


def draw_tile_reach(key, part):
    reach_values = jax.random.randint(key, (QTILES,), 1, SPAN_TILES + 1)
    near_spot = jax.random.randint(jax.random.fold_in(key, 11), (), 0, QTILES)
    far_spot = jax.random.randint(jax.random.fold_in(key, 7), (), 0, QTILES)
    reach_values = reach_values.at[near_spot].set(1)
    reach_values = reach_values.at[far_spot].set(SPAN_TILES)
    return reach_values.astype(jnp.int32)


def gain_values(key):
    return jax.random.uniform(key, (HEAD_SIZE,), jnp.float32, 0.6, 1.6)


def draw_query_gain(key, part):
    return gain_values(jax.random.fold_in(key, 5))


def draw_key_gain(key, part):
    return gain_values(jax.random.fold_in(key, 3))


def set_ends(entries, key, smallest, top_value):
    index_at = [jax.random.randint(jax.random.fold_in(key, axis), (), 0, length) for axis, length in enumerate(entries.shape)]
    widest = entries.shape.index(max(entries.shape))
    beside = index_at[:widest] + [(index_at[widest] + 1) % entries.shape[widest]] + index_at[widest + 1:]
    return entries.at[tuple(index_at)].set(smallest).at[tuple(beside)].set(top_value)


def level_of(key, dims, cuts, low, largest):
    level = 1.0
    for position, parts in cuts:
        draws = jax.random.uniform(jax.random.fold_in(jax.random.fold_in(key, 6), position), (parts,), jnp.float32, low / len(cuts), largest / len(cuts))
        level = level * jnp.repeat(jnp.exp(draws), dims[position] // parts).reshape((-1,) + (1,) * (len(dims) - 1 - position))
    return level


def profile(amount, total, bound, lean):
    weights = [(1 << 20) // math.isqrt(standing ** lean) + 1 for standing in range(2, amount + 1)]
    spare, given = total - bound - (amount - 1), [1] * (amount - 1)
    while spare > 0:
        candidates = [i for i in range(amount - 1) if given[i] < bound]
        mass, budget = sum([weights[i] for i in candidates]), spare
        for i in candidates:
            more = min(bound - given[i], max(1, budget * weights[i] // mass), spare)
            given[i] = given[i] + more
            spare = spare - more
    return np.array([bound] + given)


def uneven(own_key, count, total, bound, lean):
    if count == 2:
        one = jax.random.randint(own_key, (), max(1, total - bound), min(bound, total - 1) + 1)
        return jnp.stack([one, total - one])
    lengths = jnp.asarray(profile(count, total, bound, lean), jnp.int32)
    twos = (count - 1) // 2
    source_of, receiver = lengths[1:1 + 2 * twos:2], lengths[2:2 + 2 * twos:2]
    room = jnp.minimum(source_of - 1, bound - receiver)
    shifted = jax.random.randint(jax.random.fold_in(own_key, 1), (twos,), 0, 1 << 20) % (room + 1)
    lengths = lengths.at[1:1 + 2 * twos:2].set(source_of - shifted).at[2:2 + 2 * twos:2].set(receiver + shifted)
    return lengths[jax.random.permutation(jax.random.fold_in(own_key, 2), count)]


def centred(rng, extent, scale, bound, split=(), held_as=jnp.bfloat16):
    result = jax.random.normal(rng, extent, jnp.float32) * scale
    if len(split) > 0:
        result = level_of(rng, extent, split, -0.22, 0.18) * result
    return jnp.clip(result, min=-bound, max=bound).astype(held_as)


def setup_inputs(seed: int = 0) -> dict:
    streams_of = jax.random.split(jax.random.key(seed), 12)
    return {
        "tokens": centred(streams_of[0], (STREAM_TOKENS, MODEL_WIDTH), 1.0, 6.0, ((0, 32),)),
        "norm_gain": jnp.clip(1.0 + 0.15 * jax.random.normal(streams_of[1], (MODEL_WIDTH,), jnp.float32), 0.25, 1.75),
        "w_query": centred(streams_of[2], (MODEL_WIDTH, QUERY_HEADS * HEAD_SIZE), MODEL_WIDTH ** -0.5, 0.125, ((0, 32),)),
        "key_weight": centred(streams_of[3], (MODEL_WIDTH, KEY_VALUE_HEADS * HEAD_SIZE), MODEL_WIDTH ** -0.5, 0.125, ((0, 32),)),
        "value_weight": centred(streams_of[4], (MODEL_WIDTH, KEY_VALUE_HEADS * HEAD_SIZE), MODEL_WIDTH ** -0.5, 0.125, ((0, 32),)),
        "query_gain": draw_query_gain(jax.random.fold_in(streams_of[11], 71), 0),
        "key_gain": draw_key_gain(jax.random.fold_in(streams_of[11], 71), 0),
        "w_out": centred(streams_of[7], (QUERY_HEADS * HEAD_SIZE, MODEL_WIDTH), (QUERY_HEADS * HEAD_SIZE) ** -0.5, 0.09375, ((1, 32),)),
        "doc_ids": jnp.searchsorted(jnp.cumsum(uneven(streams_of[8], DOCS, STREAM_TOKENS, DOC_MOST, 2)), jnp.arange(STREAM_TOKENS), side="right").astype(jnp.int32),
        "sentinel": set_ends((jax.random.randint(streams_of[9], (STREAM_TOKENS,), 0, 16) < 1).astype(jnp.int32), jax.random.fold_in(streams_of[9], 1), 0, 1),
        "tile_reach": draw_tile_reach(jax.random.fold_in(streams_of[11], 71), 0),
    }


EPSILON = 1e-06
THETA = 10000000.0

def rms_norm(values, gain):
    mean_square = lax.optimization_barrier(jnp.mean(values * values, axis=-1, keepdims=True))
    return values * lax.rsqrt(mean_square + EPSILON) * gain

def rotate(values, positions):
    width = values.shape[-1]
    half_width = width // 2
    freqs = THETA ** (-2.0 * jnp.arange(half_width, dtype=jnp.float32) / width)
    angles = positions[:, None] * freqs[None, :]
    cosine = jnp.cos(angles)[:, None, :]
    sine = jnp.sin(angles)[:, None, :]
    first = values[..., :half_width]
    second = values[..., half_width:]
    return jnp.concatenate([first * cosine - second * sine, second * cosine + first * sine], axis=-1)

def reference(tokens, norm_gain, w_query, key_weight, value_weight, query_gain, key_gain, w_out, doc_ids, sentinel, tile_reach):
    normalized_rows = rms_norm(tokens.astype(jnp.float32), norm_gain).astype(jnp.bfloat16)
    positions = jnp.arange(STREAM_TOKENS, dtype=jnp.int32).astype(jnp.float32)
    query_matrix = jnp.dot(normalized_rows, w_query, preferred_element_type=jnp.float32).reshape(STREAM_TOKENS, QUERY_HEADS, HEAD_SIZE)
    query_matrix = rotate(rms_norm(query_matrix, query_gain), positions).astype(jnp.bfloat16)
    complete_keys = jnp.dot(normalized_rows, key_weight, preferred_element_type=jnp.float32).reshape(STREAM_TOKENS, KEY_VALUE_HEADS, HEAD_SIZE)
    complete_keys = rotate(rms_norm(complete_keys, key_gain), positions).astype(jnp.bfloat16)
    complete_values = jnp.dot(normalized_rows, value_weight, preferred_element_type=jnp.float32).astype(jnp.bfloat16).reshape(STREAM_TOKENS, KEY_VALUE_HEADS, HEAD_SIZE)
    tags = jnp.where(sentinel == 1, 0, doc_ids + 1).astype(jnp.int32)
    border_length = SPAN_TILES * TILE_TOKENS
    window = (SPAN_TILES + 1) * TILE_TOKENS
    head_groups = QUERY_HEADS // KEY_VALUE_HEADS
    factor_scale = 1.0 / HEAD_SIZE ** 0.5
    padded_keys = jnp.concatenate([jnp.zeros((border_length, KEY_VALUE_HEADS, HEAD_SIZE), jnp.bfloat16), complete_keys], axis=0)
    padded_values = jnp.concatenate([jnp.zeros((border_length, KEY_VALUE_HEADS, HEAD_SIZE), jnp.bfloat16), complete_values], axis=0)
    tags_pad = jnp.concatenate([jnp.zeros((border_length,), jnp.int32), tags], axis=0)

    def one_tile(tile_index):
        leading_row = (tile_index * TILE_TOKENS).astype(jnp.int32)
        query_lines = lax.dynamic_slice_in_dim(query_matrix, leading_row, TILE_TOKENS, 0).reshape(TILE_TOKENS, KEY_VALUE_HEADS, head_groups, HEAD_SIZE)
        key_rows = lax.dynamic_slice_in_dim(padded_keys, leading_row, window, 0)
        value_rows = lax.dynamic_slice_in_dim(padded_values, leading_row, window, 0)
        tag_rows = lax.dynamic_slice_in_dim(tags_pad, leading_row, window, 0)
        query_docs = lax.dynamic_slice_in_dim(doc_ids, leading_row, TILE_TOKENS, 0) + 1
        query_pos = leading_row + jnp.arange(TILE_TOKENS, dtype=jnp.int32)
        key_pos = leading_row - border_length + jnp.arange(window, dtype=jnp.int32)
        lowest = tile_index - lax.dynamic_index_in_dim(tile_reach, tile_index, 0, keepdims=False)
        same_doc = (tag_rows[None, :] == query_docs[:, None]) | (key_pos[None, :] == query_pos[:, None])
        visible = same_doc & (key_pos[None, :] <= query_pos[:, None]) & (jnp.floor_divide(key_pos, TILE_TOKENS)[None, :] >= lowest)
        scores = jnp.einsum('qcgd,kcd->cgqk', query_lines.astype(jnp.float32), key_rows.astype(jnp.float32)) * factor_scale
        scores = jnp.where(visible, scores, -jnp.inf)
        peak = lax.optimization_barrier(jnp.max(scores, axis=-1, keepdims=True))
        weights = jnp.exp(scores - peak)
        weight_total = lax.optimization_barrier(jnp.sum(weights, axis=-1))
        rounded = lax.optimization_barrier(weights.astype(jnp.bfloat16)).astype(jnp.float32)
        mixed = jnp.einsum('cgqk,kcd->qcgd', rounded, value_rows.astype(jnp.float32))
        mixed = mixed / jnp.transpose(weight_total, (2, 0, 1))[..., None]
        return mixed.astype(jnp.bfloat16).reshape(TILE_TOKENS, QUERY_HEADS * HEAD_SIZE)
    attended = lax.map(one_tile, jnp.arange(QTILES, dtype=jnp.int32)).reshape(STREAM_TOKENS, QUERY_HEADS * HEAD_SIZE)
    group_cols = QUERY_HEADS * HEAD_SIZE // N_HEAD
    summed = jnp.zeros((STREAM_TOKENS, MODEL_WIDTH), jnp.float32)
    for group in range(N_HEAD):
        partial_value = jnp.dot(attended[:, group * group_cols:(group + 1) * group_cols], w_out[group * group_cols:(group + 1) * group_cols], preferred_element_type=jnp.float32)
        summed = summed + lax.optimization_barrier(partial_value.astype(jnp.bfloat16)).astype(jnp.float32)
    return summed.astype(jnp.bfloat16)
```

```python
import functools
import math

import jax
import jax.numpy as jnp
from jax import lax
from jax.experimental import pallas as pl
from jax.experimental.pallas import tpu as pltpu
from jax.sharding import PartitionSpec as P

HEAD_SIZE = 128
TILE_TOKENS = 128
REACH_DEVS = 14


EPSILON = 1e-06
THETA = 10000000.0


def passed_along(value, axis, steps):
    count = lax.axis_size(axis)
    leading, last = (max(0, -steps), min(count, count - steps))
    return lax.ppermute(value, axis, [(source, source + steps) for source in range(leading, last)])


def rms_norm(values, gain):
    mean_square = jnp.mean(values * values, axis=-1, keepdims=True)
    return values * lax.rsqrt(mean_square + EPSILON) * gain


def rotate(values, positions):
    width = values.shape[-1]
    half_width = width // 2
    freqs = THETA ** (-2.0 * jnp.arange(half_width, dtype=jnp.float32) / width)
    angles = positions[:, None] * freqs[None, :]
    cosine = jnp.cos(angles)[:, None, :]
    sine = jnp.sin(angles)[:, None, :]
    first = values[..., :half_width]
    second = values[..., half_width:]
    return jnp.concatenate(
        [first * cosine - second * sine, second * cosine + first * sine], axis=-1
    )


def on_device(
    tokens,
    norm_gain,
    w_query,
    key_weight,
    value_weight,
    query_gain,
    key_gain,
    w_out,
    doc_ids,
    sentinel,
    tile_reach,
):
    whole = lax.all_gather(tokens, "head", axis=1, tiled=True)
    row_count = whole.shape[0]
    normalized_rows = rms_norm(whole.astype(jnp.float32), norm_gain).astype(jnp.bfloat16)
    query_cols = w_query.shape[1]
    key_cols = key_weight.shape[1]
    portions = (
        lax.all_gather(w_query, "tok", axis=0, tiled=True),
        lax.all_gather(key_weight, "tok", axis=0, tiled=True),
        lax.all_gather(value_weight, "tok", axis=0, tiled=True),
    )
    proj_query, proj_key, proj_value = tuple(
        (
            jnp.dot(normalized_rows, portion, preferred_element_type=jnp.float32)
            for portion in portions
        )
    )
    base_row = lax.axis_index("tok") * row_count
    positions = (base_row + jnp.arange(row_count, dtype=jnp.int32)).astype(jnp.float32)
    local_heads = query_cols // HEAD_SIZE
    local_kv = key_cols // HEAD_SIZE
    head_groups = local_heads // local_kv
    query_matrix = rotate(
        rms_norm(proj_query.reshape(row_count, local_heads, HEAD_SIZE), query_gain), positions
    )
    query_matrix = query_matrix.astype(jnp.bfloat16).reshape(
        row_count, local_kv, head_groups, HEAD_SIZE
    )
    keys_own = rotate(
        rms_norm(proj_key.reshape(row_count, local_kv, HEAD_SIZE), key_gain), positions
    ).astype(jnp.bfloat16)
    values_own = proj_value.astype(jnp.bfloat16).reshape(row_count, local_kv, HEAD_SIZE)
    tags_own = jnp.where(sentinel == 1, 0, doc_ids + 1).astype(jnp.bfloat16)
    blocks = REACH_DEVS + 1

    def pass_along(step_index, state):
        current, key_store, value_store, tag_store = state
        current = passed_along((current[0], current[1], current[2]), "tok", 1)
        slot = REACH_DEVS - 1 - step_index
        key_store = lax.dynamic_update_index_in_dim(key_store, current[0], slot, 0)
        value_store = lax.dynamic_update_index_in_dim(value_store, current[1], slot, 0)
        tag_store = lax.dynamic_update_index_in_dim(tag_store, current[2], slot, 0)
        return (current, key_store, value_store, tag_store)

    key_store = (
        jnp.zeros((blocks, row_count, local_kv, HEAD_SIZE), jnp.bfloat16)
        .at[REACH_DEVS]
        .set(keys_own)
    )
    value_store = (
        jnp.zeros((blocks, row_count, local_kv, HEAD_SIZE), jnp.bfloat16)
        .at[REACH_DEVS]
        .set(values_own)
    )
    tag_store = jnp.zeros((blocks, row_count), jnp.bfloat16).at[REACH_DEVS].set(tags_own)
    state = lax.fori_loop(
        0,
        REACH_DEVS,
        pass_along,
        ((keys_own, values_own, tags_own), key_store, value_store, tag_store),
    )
    key_store, value_store, tag_store = (state[1], state[2], state[3])
    factor_scale = 1.0 / math.sqrt(HEAD_SIZE)
    outputs = []
    for tile_index in range(row_count // TILE_TOKENS):
        query_tile = query_matrix[tile_index * TILE_TOKENS : (tile_index + 1) * TILE_TOKENS]
        query_pos = base_row + tile_index * TILE_TOKENS + jnp.arange(TILE_TOKENS, dtype=jnp.int32)
        query_docs = doc_ids[tile_index * TILE_TOKENS : (tile_index + 1) * TILE_TOKENS] + 1
        lowest = base_row // TILE_TOKENS + tile_index - tile_reach[tile_index]

        def update(
            block,
            state,
            query_tile=query_tile,
            query_pos=query_pos,
            query_docs=query_docs,
            lowest=lowest,
        ):
            key_block = key_store[block]
            value_block = value_store[block]
            tag_block = tag_store[block].astype(jnp.int32)
            key_pos = (
                base_row + (block - REACH_DEVS) * row_count + jnp.arange(row_count, dtype=jnp.int32)
            )
            same_doc = (tag_block[None, :] == query_docs[:, None]) | (
                key_pos[None, :] == query_pos[:, None]
            )
            visible = (
                same_doc
                & (key_pos[None, :] <= query_pos[:, None])
                & (jnp.floor_divide(key_pos, TILE_TOKENS)[None, :] >= lowest)
            )

            def compute(inner):
                peak_run, weight_sum, accum_out = inner
                scores = (
                    jnp.einsum(
                        "qcgd,kcd->cgqk", query_tile, key_block, preferred_element_type=jnp.float32
                    )
                    * factor_scale
                )
                scores = jnp.where(visible, scores, -jnp.inf)
                peak_new = jnp.maximum(peak_run, jnp.max(scores, axis=-1))
                shrink = jnp.exp(peak_run - peak_new)
                weights = jnp.exp(scores - peak_new[..., None])
                weight_sum = weight_sum * shrink + jnp.sum(weights, axis=-1)
                mixed = jnp.einsum(
                    "cgqk,kcd->cgqd",
                    weights.astype(jnp.bfloat16),
                    value_block,
                    preferred_element_type=jnp.float32,
                )
                return (peak_new, weight_sum, accum_out * shrink[..., None] + mixed)

            return lax.cond(jnp.any(visible), compute, lambda inner: inner, state)

        initial = (
            jnp.full((local_kv, head_groups, TILE_TOKENS), -1e30, jnp.float32),
            jnp.zeros((local_kv, head_groups, TILE_TOKENS), jnp.float32),
            jnp.zeros((local_kv, head_groups, TILE_TOKENS, HEAD_SIZE), jnp.float32),
        )
        peak_run, weight_sum, accum_out = lax.fori_loop(0, blocks, update, initial)
        result = accum_out / weight_sum[..., None]
        outputs.append(
            jnp.transpose(result, (2, 0, 1, 3))
            .reshape(TILE_TOKENS, query_cols)
            .astype(jnp.bfloat16)
        )
    attended = jnp.concatenate(outputs, axis=0)
    partials = jnp.dot(
        attended,
        lax.all_gather(w_out, "tok", axis=1, tiled=True),
        preferred_element_type=jnp.float32,
    )
    return lax.psum_scatter(partials.astype(jnp.bfloat16), "head", scatter_dimension=1, tiled=True)


CHUNK = 512
MESH_IDS = pl.DeviceIdType.MESH
MASKED = -1e30


def send(source, target, send_sem, recv_sem, device):
    return pltpu.make_async_remote_copy(
        src_ref=source,
        dst_ref=target,
        send_sem=send_sem,
        recv_sem=recv_sem,
        device_id={"tok": device},
        device_id_type=MESH_IDS,
    )


def head_norm_rotate(values, gain, cosine, sine):
    mean_square = jnp.mean(values * values, axis=-1, keepdims=True)
    normed = values * lax.rsqrt(mean_square + EPSILON) * gain
    return normed * cosine + pltpu.roll(normed, HEAD_SIZE // 2, 1) * sine


def project_kernel(
    members,
    groups,
    reach_rows,
    normed_ref,
    pack_ref,
    out_pack_ref,
    cos_ref,
    sin_ref,
    query_gain_ref,
    key_gain_ref,
    query_ref,
    window_ref,
    out_block_ref,
    rows_all,
    weights_all,
    kv_own,
    own_sems,
    pack_send,
    pack_recv,
    out_send,
    out_recv,
    row_send,
    row_recv,
    block_send,
    block_recv,
    kv_send,
    kv_recv,
):
    me = lax.axis_index("tok")
    g = lax.rem(me, members)
    t = lax.div(me, members)
    y = lax.rem(t, 2)
    z = lax.div(t, 2)
    depth_z = groups // 2
    base = t * members
    side = me + members * (1 - 2 * y)
    below, above = me - 2 * members, me + 2 * members
    row_count = normed_ref.shape[0]
    group_rows = members * row_count
    back = -(-reach_rows // group_rows)
    window_rows = window_ref.shape[0]

    barrier = pltpu.get_barrier_semaphore()
    for step in range(1, members):
        other = base + lax.rem(g + step, members)
        pl.semaphore_signal(barrier, inc=1, device_id={"tok": other}, device_id_type=MESH_IDS)
    span = max(back, 2)
    peers = members - 1
    for delta in [*range(-span, 0), *range(1, span + 1)]:
        present = (t + delta >= 0) & (t + delta < groups)
        peers = peers + present.astype(jnp.int32)

        @pl.when(present)
        def _(delta=delta):
            pl.semaphore_signal(
                barrier, inc=1, device_id={"tok": me + delta * members}, device_id_type=MESH_IDS
            )

    pl.semaphore_wait(barrier, peers)

    own = [
        pltpu.make_async_copy(pack_ref.at[g], weights_all.at[t, g], own_sems.at[0]),
        pltpu.make_async_copy(out_pack_ref.at[g], out_block_ref.at[g], own_sems.at[1]),
        pltpu.make_async_copy(normed_ref, rows_all.at[g], own_sems.at[2]),
    ]

    def pack_copy(step):
        j = lax.rem(g + step, members)
        return send(
            pack_ref.at[j], weights_all.at[t, g], pack_send.at[step], pack_recv.at[step], base + j
        )

    def out_copy(step):
        j = lax.rem(g + step, members)
        return send(
            out_pack_ref.at[j], out_block_ref.at[g], out_send.at[step], out_recv.at[step], base + j
        )

    partner = base + g + 1 - 2 * lax.rem(g, 2)
    across_g = lax.rem(g + 2, members)
    across = base + across_g
    row_copies = [
        send(normed_ref, rows_all.at[g], row_send.at[0], row_recv.at[0], partner),
        send(normed_ref, rows_all.at[g], row_send.at[1], row_recv.at[1], across),
        send(rows_all.at[across_g], rows_all.at[across_g], row_send.at[2], row_recv.at[2], partner),
    ]
    for copy in own:
        copy.start()
    for step in range(1, members):
        pack_copy(step).start()
    row_copies[1].start()
    row_copies[0].start()
    for step in range(1, members):
        pack_copy(step).wait_recv()
    own[0].wait()

    def block_copy(block, way, device):
        return send(
            weights_all.at[block],
            weights_all.at[block],
            block_send.at[block, way],
            block_recv.at[block],
            device,
        )

    def forward(block, up, down):
        if up:

            @pl.when(z < depth_z - 1)
            def _():
                block_copy(block, 0, above).start()

        if down:

            @pl.when(z > 0)
            def _():
                block_copy(block, 1, below).start()

        block_copy(block, 2, side).start()

    def forward_done(block, up, down):
        if up:

            @pl.when(z < depth_z - 1)
            def _():
                block_copy(block, 0, above).wait_send()

        if down:

            @pl.when(z > 0)
            def _():
                block_copy(block, 1, below).wait_send()

        block_copy(block, 2, side).wait_send()

    forward(t, True, True)
    for step in range(1, members):
        out_copy(step).start()
    row_copies[1].wait_recv()
    row_copies[2].start()
    for k in range(1, depth_z):

        @pl.when(z >= k)
        def _(k=k):
            block_copy(t - 2 * k, 0, above).wait_recv()
            forward(t - 2 * k, True, False)

        @pl.when(z + k < depth_z)
        def _(k=k):
            block_copy(t + 2 * k, 1, below).wait_recv()
            forward(t + 2 * k, False, True)

    row_copies[0].wait_recv()
    row_copies[2].wait_recv()
    own[1].wait()
    own[2].wait()
    for k in range(depth_z):
        block_copy(2 * k + 1 - y, 2, side).wait_recv()

    model = weights_all.shape[1] * weights_all.shape[2] * groups
    columns = weights_all.shape[3]
    query_cols = columns - 2 * HEAD_SIZE
    share = row_count
    width_k = model // groups

    def project(member, start, size):
        def add(block, total):
            piece = rows_all[member, :, pl.ds(pl.multiple_of(block * width_k, width_k), width_k)]
            weight = weights_all[block, :, :, pl.ds(start, size)].reshape(width_k, size)
            return total + jnp.dot(piece, weight, preferred_element_type=jnp.float32)

        total = jnp.zeros((row_count, size), jnp.float32)
        return lax.fori_loop(0, groups, add, total, unroll=True)

    @pl.loop(0, members)
    def _(member):
        rows = pl.ds(pl.multiple_of(member * share, share), share)
        both = project(member, query_cols, 2 * HEAD_SIZE)
        key = head_norm_rotate(
            both[:, :HEAD_SIZE], key_gain_ref[...], cos_ref[rows, :], sin_ref[rows, :]
        )
        kv_own[rows, :HEAD_SIZE] = key.astype(jnp.bfloat16)
        kv_own[rows, HEAD_SIZE:] = both[:, HEAD_SIZE:].astype(jnp.bfloat16)

    def slot(distance):
        full = window_rows - (distance + 1) * group_rows
        low = window_rows - group_rows - reach_rows
        skip = max(0, low - full)
        return skip, full + skip

    def kv_copy(distance):
        skip, start = slot(distance)
        return send(
            kv_own.at[pl.ds(skip, group_rows - skip)],
            window_ref.at[pl.ds(start, group_rows - skip)],
            kv_send.at[distance - 1],
            kv_recv.at[distance - 1],
            me + distance * members,
        )

    for distance in range(back, 0, -1):

        @pl.when(t + distance < groups)
        def _(distance=distance):
            kv_copy(distance).start()

        @pl.when(t < distance)
        def _(distance=distance):
            skip, start = slot(distance)
            window_ref[start : start + group_rows - skip, :] = jnp.zeros(
                (group_rows - skip, 2 * HEAD_SIZE), jnp.bfloat16
            )

    pad = window_rows - group_rows - reach_rows
    window_ref[:pad, :] = jnp.zeros((pad, 2 * HEAD_SIZE), jnp.bfloat16)

    pair = 2 * HEAD_SIZE

    @pl.loop(0, members)
    def _(member):
        rows = pl.ds(pl.multiple_of(member * share, share), share)
        window_ref[pl.ds(pl.multiple_of(window_rows - group_rows + member * share, 128), share), :] = kv_own[rows, :]

        @pl.loop(0, query_cols // pair)
        def _(h):
            both = project(member, pl.multiple_of(h * pair, pair), pair)
            for half in range(2):
                head = head_norm_rotate(
                    both[:, half * HEAD_SIZE : (half + 1) * HEAD_SIZE],
                    query_gain_ref[...],
                    cos_ref[rows, :],
                    sin_ref[rows, :],
                )
                query_ref[2 * h + half, rows, :] = head.astype(jnp.bfloat16)

    for distance in range(1, back + 1):

        @pl.when(t >= distance)
        def _(distance=distance):
            kv_copy(distance).wait_recv()

        @pl.when(t + distance < groups)
        def _(distance=distance):
            kv_copy(distance).wait_send()

    for step in range(1, members):
        pack_copy(step).wait_send()
        out_copy(step).wait()
    for copy in row_copies:
        copy.wait_send()
    forward_done(t, True, True)
    for k in range(1, depth_z):

        @pl.when(z >= k)
        def _(k=k):
            forward_done(t - 2 * k, True, False)

        @pl.when(z + k < depth_z)
        def _(k=k):
            forward_done(t + 2 * k, False, True)


def attention_kernel(counts, floors, query_ref, docs_ref, window_ref, tags_ref, out_ref, acc, peak, total):
    tile = pl.program_id(0)
    heads = query_ref.shape[0]
    window_rows = window_ref.shape[0]
    tiles = pl.num_programs(0)
    end = window_rows - (tiles - 1 - tile) * TILE_TOKENS
    factor = math.log2(math.e) / math.sqrt(HEAD_SIZE)
    query_at = end - TILE_TOKENS + lax.broadcasted_iota(jnp.int32, (TILE_TOKENS, CHUNK), 0)
    peak[...] = jnp.full_like(peak, MASKED)
    total[...] = jnp.zeros_like(total)
    acc[...] = jnp.zeros_like(acc)

    @pl.loop(0, counts[tile])
    def _(step):
        start = pl.multiple_of(end - (step + 1) * CHUNK, TILE_TOKENS)
        keys = window_ref[pl.ds(start, CHUNK), :HEAD_SIZE]
        values = window_ref[pl.ds(start, CHUNK), HEAD_SIZE:]
        key_at = start + lax.broadcasted_iota(jnp.int32, (TILE_TOKENS, CHUNK), 1)
        tags = tags_ref[:, pl.ds(start, CHUNK)]
        visible = (
            ((tags == docs_ref[...]) | (key_at == query_at))
            & (key_at <= query_at)
            & (key_at >= floors[tile])
        )
        for h in range(heads):
            scores = lax.dot_general(
                query_ref[h], keys, (((1,), (1,)), ((), ())), preferred_element_type=jnp.float32
            )
            scores = jnp.where(visible, scores * factor, MASKED)
            before = peak[h]
            now = jnp.maximum(before, jnp.max(scores, axis=-1, keepdims=True))
            shrink = jnp.exp2(before - now)
            weights = jnp.exp2(scores - now[:, :1])
            total[h] = total[h] * shrink + jnp.sum(weights, axis=-1, keepdims=True)
            acc[h] = acc[h] * shrink + jnp.dot(
                weights.astype(jnp.bfloat16), values, preferred_element_type=jnp.float32
            )
            peak[h] = now

    for h in range(heads):
        out_ref[:, h * HEAD_SIZE : (h + 1) * HEAD_SIZE] = (acc[h] / total[h]).astype(jnp.bfloat16)


def output_kernel(
    members,
    attended_ref,
    weight_ref,
    out_ref,
    near_out,
    near_in,
    far_out,
    far_in,
    near_send,
    near_recv,
    far_send,
    far_recv,
):
    me = lax.axis_index("tok")
    g = lax.rem(me, members)
    base = me - g
    core = lax.rem(g, 2)
    partner_g = g + 1 - 2 * core
    across_g = lax.rem(g + 2, members)
    diagonal_g = lax.rem(partner_g + 2, members)
    partner, across = base + partner_g, base + across_g
    row_count = out_ref.shape[0]
    pieces = near_out.shape[1]
    width = near_out.shape[3]
    barrier = pltpu.get_barrier_semaphore()
    for other in (partner, across):
        pl.semaphore_signal(barrier, inc=1, device_id={"tok": other}, device_id_type=MESH_IDS)
    pl.semaphore_wait(barrier, 2)

    def partial(member, piece):
        rows = pl.ds(pl.multiple_of(member * row_count, row_count), row_count)
        return lax.dot_general(
            attended_ref[rows, :],
            weight_ref[piece * width : (piece + 1) * width, :],
            (((1,), (1,)), ((), ())),
            preferred_element_type=jnp.float32,
        )

    def near(way, piece):
        return send(
            near_out.at[way, piece],
            near_in.at[way, piece],
            near_send.at[way, piece],
            near_recv.at[way, piece],
            partner,
        )

    def far(piece):
        return send(
            far_out.at[piece], far_in.at[piece], far_send.at[piece], far_recv.at[piece], across
        )

    for piece in range(pieces):
        near_out[0, piece] = partial(diagonal_g, piece).astype(jnp.bfloat16)
        near(0, piece).start()
    for piece in range(pieces):
        mine = partial(across_g, piece).astype(jnp.bfloat16).astype(jnp.float32)
        near(0, piece).wait_recv()
        far_out[piece] = (mine + near_in[0, piece].astype(jnp.float32)).astype(jnp.bfloat16)
        far(piece).start()
    for piece in range(pieces):
        near_out[1, piece] = partial(partner_g, piece).astype(jnp.bfloat16)
        near(1, piece).start()
    for piece in range(pieces):
        mine = partial(g, piece).astype(jnp.bfloat16).astype(jnp.float32)
        near(1, piece).wait_recv()
        mine = mine + near_in[1, piece].astype(jnp.float32)
        far(piece).wait_recv()
        out_ref[:, piece * width : (piece + 1) * width] = (
            mine + far_in[piece].astype(jnp.float32)
        ).astype(jnp.bfloat16)
    for piece in range(pieces):
        near(0, piece).wait_send()
        near(1, piece).wait_send()
        far(piece).wait_send()


VMEM_BYTES = 60 << 20


def in_vmem(count):
    return [pl.BlockSpec(memory_space=pltpu.VMEM)] * count


def grouped(
    tokens,
    norm_gain,
    w_query,
    key_weight,
    value_weight,
    query_gain,
    key_gain,
    w_out,
    doc_ids,
    sentinel,
    tile_reach,
):
    row_count = tokens.shape[0]
    depth = w_query.shape[0]
    members = key_weight.shape[1] // HEAD_SIZE
    devices = lax.axis_size("tok")
    groups = devices // members
    group_rows = members * row_count
    reach_rows = REACH_DEVS * row_count
    pad = CHUNK - TILE_TOKENS
    window_rows = pad + reach_rows + group_rows
    query_cols = w_query.shape[1] // members
    heads = query_cols // HEAD_SIZE
    model = tokens.shape[1]
    group = lax.axis_index("tok") // members
    base_row = group * group_rows

    facts = jnp.concatenate([doc_ids, sentinel, jnp.pad(tile_reach, (0, 128 - tile_reach.shape[0]))])
    facts = lax.all_gather(facts, "tok", axis=0, tiled=False)

    normed = rms_norm(tokens.astype(jnp.float32), norm_gain).astype(jnp.bfloat16)
    pack = jnp.concatenate(
        [
            w_query.reshape(depth, members, query_cols),
            key_weight.reshape(depth, members, HEAD_SIZE),
            value_weight.reshape(depth, members, HEAD_SIZE),
        ],
        axis=2,
    ).transpose(1, 0, 2)
    out_depth = w_out.shape[1]
    out_pack = w_out.T.reshape(out_depth, members, query_cols).transpose(1, 0, 2)
    positions = (base_row + jnp.arange(group_rows, dtype=jnp.int32)).astype(jnp.float32)
    half_width = HEAD_SIZE // 2
    freqs = THETA ** (-2.0 * jnp.arange(half_width, dtype=jnp.float32) / HEAD_SIZE)
    angles = positions[:, None] * freqs[None, :]
    cosine, sine = jnp.cos(angles), jnp.sin(angles)
    cosine = jnp.concatenate([cosine, cosine], axis=1)
    sine = jnp.concatenate([-sine, sine], axis=1)
    columns = query_cols + 2 * HEAD_SIZE
    back = -(-reach_rows // group_rows)
    dma = pltpu.SemaphoreType.DMA
    queries, window, out_block = pl.pallas_call(
        functools.partial(project_kernel, members, groups, reach_rows),
        out_shape=(
            jax.ShapeDtypeStruct((heads, group_rows, HEAD_SIZE), jnp.bfloat16),
            jax.ShapeDtypeStruct((window_rows, 2 * HEAD_SIZE), jnp.bfloat16),
            jax.ShapeDtypeStruct((members, out_depth, query_cols), jnp.bfloat16),
        ),
        in_specs=in_vmem(7),
        out_specs=tuple(in_vmem(3)),
        scratch_shapes=[
            pltpu.VMEM((members, row_count, model), jnp.bfloat16),
            pltpu.VMEM((groups, members, depth, columns), jnp.bfloat16),
            pltpu.VMEM((group_rows, 2 * HEAD_SIZE), jnp.bfloat16),
            dma((3,)),
            dma((members,)),
            dma((members,)),
            dma((members,)),
            dma((members,)),
            dma((3,)),
            dma((3,)),
            dma((groups, 3)),
            dma((groups,)),
            dma((back,)),
            dma((back,)),
        ],
        compiler_params=pltpu.CompilerParams(
            collective_id=0, has_side_effects=True, vmem_limit_bytes=VMEM_BYTES
        ),
        name="project",
    )(normed, pack, out_pack, cosine, sine, query_gain[None, :], key_gain[None, :])

    out_weight = lax.all_gather(
        out_block.reshape(members * out_depth, query_cols),
        "tok",
        axis=0,
        tiled=True,
        axis_index_groups=[
            [step * members + member for step in range(groups)] for member in range(members)
        ],
    )

    docs_all = facts[:, :row_count].reshape(-1)
    tags_all = jnp.where(facts[:, row_count : 2 * row_count].reshape(-1) == 1, 0, docs_all + 1)
    tiles_each = tile_reach.shape[0]
    reach_all = facts[:, 2 * row_count : 2 * row_count + tiles_each].reshape(-1)
    tiles = group_rows // TILE_TOKENS
    missing = pad + reach_rows
    tags_window = lax.dynamic_slice_in_dim(
        jnp.pad(tags_all, (missing, 0), constant_values=-1), base_row, window_rows
    )[None, :]
    query_docs = lax.dynamic_slice_in_dim(docs_all, base_row, group_rows)
    reach = lax.dynamic_slice_in_dim(reach_all, group * tiles, tiles)
    offset = base_row - missing
    tile_start = base_row + jnp.arange(tiles, dtype=jnp.int32) * TILE_TOKENS
    first_doc = query_docs[::TILE_TOKENS]
    doc_start = jnp.sum((docs_all[None, :] < first_doc[:, None]).astype(jnp.int32), axis=1)
    floor_row = jnp.maximum(tile_start - reach * TILE_TOKENS, 0)
    lowest = jnp.maximum(floor_row, doc_start // TILE_TOKENS * TILE_TOKENS)
    counts = (tile_start + TILE_TOKENS - lowest + CHUNK - 1) // CHUNK
    floors = floor_row - offset

    attended = pl.pallas_call(
        attention_kernel,
        out_shape=jax.ShapeDtypeStruct((group_rows, query_cols), jnp.bfloat16),
        grid_spec=pltpu.PrefetchScalarGridSpec(
            num_scalar_prefetch=2,
            grid=(tiles,),
            in_specs=[
                pl.BlockSpec((heads, TILE_TOKENS, HEAD_SIZE), lambda i, *_: (0, i, 0)),
                pl.BlockSpec((TILE_TOKENS, 1), lambda i, *_: (i, 0)),
                pl.BlockSpec((window_rows, 2 * HEAD_SIZE), lambda i, *_: (0, 0)),
                pl.BlockSpec((1, window_rows), lambda i, *_: (0, 0)),
            ],
            out_specs=pl.BlockSpec((TILE_TOKENS, query_cols), lambda i, *_: (i, 0)),
            scratch_shapes=[pltpu.VMEM((heads, TILE_TOKENS, HEAD_SIZE), jnp.float32)] * 3,
        ),
        compiler_params=pltpu.CompilerParams(vmem_limit_bytes=VMEM_BYTES),
        cost_estimate=pl.CostEstimate(
            flops=2 * group_rows * window_rows * query_cols,
            bytes_accessed=window_rows * 4 * HEAD_SIZE + 4 * group_rows * query_cols,
            transcendentals=group_rows * window_rows * heads // 2,
        ),
        name="attend",
    )(counts, floors, queries, query_docs[:, None] + 1, window, tags_window)

    pieces = 4
    width = model // pieces
    return pl.pallas_call(
        functools.partial(output_kernel, members),
        out_shape=jax.ShapeDtypeStruct((row_count, model), jnp.bfloat16),
        in_specs=in_vmem(2),
        out_specs=in_vmem(1)[0],
        scratch_shapes=[
            pltpu.VMEM((2, pieces, row_count, width), jnp.bfloat16),
            pltpu.VMEM((2, pieces, row_count, width), jnp.bfloat16),
            pltpu.VMEM((pieces, row_count, width), jnp.bfloat16),
            pltpu.VMEM((pieces, row_count, width), jnp.bfloat16),
            dma((2, pieces)),
            dma((2, pieces)),
            dma((pieces,)),
            dma((pieces,)),
        ],
        compiler_params=pltpu.CompilerParams(
            collective_id=1, has_side_effects=True, vmem_limit_bytes=VMEM_BYTES
        ),
        name="output",
    )(attended, out_weight)


def chosen(*arguments):
    members = arguments[3].shape[1] // HEAD_SIZE
    devices = lax.axis_size("tok")
    if lax.axis_size("head") == 1 and members == 4 and devices % (2 * members) == 0:
        return grouped(*arguments)
    return on_device(*arguments)


def solution(mesh):
    return jax.shard_map(
        chosen,
        mesh=mesh,
        in_specs=(
            P("tok", "head"),
            P(),
            P("tok", "head"),
            P("tok", "head"),
            P("tok", "head"),
            P(),
            P(),
            P("head", "tok"),
            P("tok"),
            P("tok"),
            P("tok"),
        ),
        out_specs=P("tok", "head"),
        check_vma=False,
    )
```

```python
import functools
import math

import jax
import jax.numpy as jnp
from jax import lax
from jax.experimental import pallas as pl
from jax.experimental.pallas import tpu as pltpu
from jax.sharding import PartitionSpec as P

HEAD_SIZE = 128
TILE_TOKENS = 128
REACH_DEVS = 14


EPSILON = 1e-06
THETA = 10000000.0


def passed_along(value, axis, steps):
    count = lax.axis_size(axis)
    leading, last = (max(0, -steps), min(count, count - steps))
    return lax.ppermute(value, axis, [(source, source + steps) for source in range(leading, last)])


def rms_norm(values, gain):
    mean_square = jnp.mean(values * values, axis=-1, keepdims=True)
    return values * lax.rsqrt(mean_square + EPSILON) * gain


def rotate(values, positions):
    width = values.shape[-1]
    half_width = width // 2
    freqs = THETA ** (-2.0 * jnp.arange(half_width, dtype=jnp.float32) / width)
    angles = positions[:, None] * freqs[None, :]
    cosine = jnp.cos(angles)[:, None, :]
    sine = jnp.sin(angles)[:, None, :]
    first = values[..., :half_width]
    second = values[..., half_width:]
    return jnp.concatenate(
        [first * cosine - second * sine, second * cosine + first * sine], axis=-1
    )


def on_device(
    tokens,
    norm_gain,
    w_query,
    key_weight,
    value_weight,
    query_gain,
    key_gain,
    w_out,
    doc_ids,
    sentinel,
    tile_reach,
):
    whole = lax.all_gather(tokens, "head", axis=1, tiled=True)
    row_count = whole.shape[0]
    normalized_rows = rms_norm(whole.astype(jnp.float32), norm_gain).astype(jnp.bfloat16)
    query_cols = w_query.shape[1]
    key_cols = key_weight.shape[1]
    portions = (
        lax.all_gather(w_query, "tok", axis=0, tiled=True),
        lax.all_gather(key_weight, "tok", axis=0, tiled=True),
        lax.all_gather(value_weight, "tok", axis=0, tiled=True),
    )
    proj_query, proj_key, proj_value = tuple(
        (
            jnp.dot(normalized_rows, portion, preferred_element_type=jnp.float32)
            for portion in portions
        )
    )
    base_row = lax.axis_index("tok") * row_count
    positions = (base_row + jnp.arange(row_count, dtype=jnp.int32)).astype(jnp.float32)
    local_heads = query_cols // HEAD_SIZE
    local_kv = key_cols // HEAD_SIZE
    head_groups = local_heads // local_kv
    query_matrix = rotate(
        rms_norm(proj_query.reshape(row_count, local_heads, HEAD_SIZE), query_gain), positions
    )
    query_matrix = query_matrix.astype(jnp.bfloat16).reshape(
        row_count, local_kv, head_groups, HEAD_SIZE
    )
    keys_own = rotate(
        rms_norm(proj_key.reshape(row_count, local_kv, HEAD_SIZE), key_gain), positions
    ).astype(jnp.bfloat16)
    values_own = proj_value.astype(jnp.bfloat16).reshape(row_count, local_kv, HEAD_SIZE)
    tags_own = jnp.where(sentinel == 1, 0, doc_ids + 1).astype(jnp.bfloat16)
    blocks = REACH_DEVS + 1

    def pass_along(step_index, state):
        current, key_store, value_store, tag_store = state
        current = passed_along((current[0], current[1], current[2]), "tok", 1)
        slot = REACH_DEVS - 1 - step_index
        key_store = lax.dynamic_update_index_in_dim(key_store, current[0], slot, 0)
        value_store = lax.dynamic_update_index_in_dim(value_store, current[1], slot, 0)
        tag_store = lax.dynamic_update_index_in_dim(tag_store, current[2], slot, 0)
        return (current, key_store, value_store, tag_store)

    key_store = (
        jnp.zeros((blocks, row_count, local_kv, HEAD_SIZE), jnp.bfloat16)
        .at[REACH_DEVS]
        .set(keys_own)
    )
    value_store = (
        jnp.zeros((blocks, row_count, local_kv, HEAD_SIZE), jnp.bfloat16)
        .at[REACH_DEVS]
        .set(values_own)
    )
    tag_store = jnp.zeros((blocks, row_count), jnp.bfloat16).at[REACH_DEVS].set(tags_own)
    state = lax.fori_loop(
        0,
        REACH_DEVS,
        pass_along,
        ((keys_own, values_own, tags_own), key_store, value_store, tag_store),
    )
    key_store, value_store, tag_store = (state[1], state[2], state[3])
    factor_scale = 1.0 / math.sqrt(HEAD_SIZE)
    outputs = []
    for tile_index in range(row_count // TILE_TOKENS):
        query_tile = query_matrix[tile_index * TILE_TOKENS : (tile_index + 1) * TILE_TOKENS]
        query_pos = base_row + tile_index * TILE_TOKENS + jnp.arange(TILE_TOKENS, dtype=jnp.int32)
        query_docs = doc_ids[tile_index * TILE_TOKENS : (tile_index + 1) * TILE_TOKENS] + 1
        lowest = base_row // TILE_TOKENS + tile_index - tile_reach[tile_index]

        def update(
            block,
            state,
            query_tile=query_tile,
            query_pos=query_pos,
            query_docs=query_docs,
            lowest=lowest,
        ):
            key_block = key_store[block]
            value_block = value_store[block]
            tag_block = tag_store[block].astype(jnp.int32)
            key_pos = (
                base_row + (block - REACH_DEVS) * row_count + jnp.arange(row_count, dtype=jnp.int32)
            )
            same_doc = (tag_block[None, :] == query_docs[:, None]) | (
                key_pos[None, :] == query_pos[:, None]
            )
            visible = (
                same_doc
                & (key_pos[None, :] <= query_pos[:, None])
                & (jnp.floor_divide(key_pos, TILE_TOKENS)[None, :] >= lowest)
            )

            def compute(inner):
                peak_run, weight_sum, accum_out = inner
                scores = (
                    jnp.einsum(
                        "qcgd,kcd->cgqk", query_tile, key_block, preferred_element_type=jnp.float32
                    )
                    * factor_scale
                )
                scores = jnp.where(visible, scores, -jnp.inf)
                peak_new = jnp.maximum(peak_run, jnp.max(scores, axis=-1))
                shrink = jnp.exp(peak_run - peak_new)
                weights = jnp.exp(scores - peak_new[..., None])
                weight_sum = weight_sum * shrink + jnp.sum(weights, axis=-1)
                mixed = jnp.einsum(
                    "cgqk,kcd->cgqd",
                    weights.astype(jnp.bfloat16),
                    value_block,
                    preferred_element_type=jnp.float32,
                )
                return (peak_new, weight_sum, accum_out * shrink[..., None] + mixed)

            return lax.cond(jnp.any(visible), compute, lambda inner: inner, state)

        initial = (
            jnp.full((local_kv, head_groups, TILE_TOKENS), -1e30, jnp.float32),
            jnp.zeros((local_kv, head_groups, TILE_TOKENS), jnp.float32),
            jnp.zeros((local_kv, head_groups, TILE_TOKENS, HEAD_SIZE), jnp.float32),
        )
        peak_run, weight_sum, accum_out = lax.fori_loop(0, blocks, update, initial)
        result = accum_out / weight_sum[..., None]
        outputs.append(
            jnp.transpose(result, (2, 0, 1, 3))
            .reshape(TILE_TOKENS, query_cols)
            .astype(jnp.bfloat16)
        )
    attended = jnp.concatenate(outputs, axis=0)
    partials = jnp.dot(
        attended,
        lax.all_gather(w_out, "tok", axis=1, tiled=True),
        preferred_element_type=jnp.float32,
    )
    return lax.psum_scatter(partials.astype(jnp.bfloat16), "head", scatter_dimension=1, tiled=True)


CHUNK = 512
MESH_IDS = pl.DeviceIdType.MESH
MASKED = -1e30


def send(source, target, send_sem, recv_sem, device):
    return pltpu.make_async_remote_copy(
        src_ref=source,
        dst_ref=target,
        send_sem=send_sem,
        recv_sem=recv_sem,
        device_id={"tok": device},
        device_id_type=MESH_IDS,
    )


def head_norm_rotate(values, gain, cosine, sine):
    mean_square = jnp.mean(values * values, axis=-1, keepdims=True)
    normed = values * lax.rsqrt(mean_square + EPSILON) * gain
    return normed * cosine + pltpu.roll(normed, HEAD_SIZE // 2, 1) * sine


def project_kernel(
    members,
    groups,
    reach_rows,
    normed_ref,
    pack_ref,
    out_pack_ref,
    cos_ref,
    sin_ref,
    query_gain_ref,
    key_gain_ref,
    facts_ref,
    query_ref,
    window_ref,
    out_block_ref,
    facts_window_ref,
    rows_all,
    weights_all,
    kv_own,
    own_sems,
    pack_send,
    pack_recv,
    out_send,
    out_recv,
    row_send,
    row_recv,
    block_send,
    block_recv,
    kv_send,
    kv_recv,
    fact_send,
    fact_recv,
    past_send,
    past_recv,
):
    me = lax.axis_index("tok")
    g = lax.rem(me, members)
    t = lax.div(me, members)
    y = lax.rem(t, 2)
    z = lax.div(t, 2)
    depth_z = groups // 2
    base = t * members
    side = me + members * (1 - 2 * y)
    below, above = me - 2 * members, me + 2 * members
    row_count = normed_ref.shape[0]
    group_rows = members * row_count
    back = -(-reach_rows // group_rows)
    window_rows = window_ref.shape[0]

    barrier = pltpu.get_barrier_semaphore()
    for step in range(1, members):
        other = base + lax.rem(g + step, members)
        pl.semaphore_signal(barrier, inc=1, device_id={"tok": other}, device_id_type=MESH_IDS)
    span = max(back, 2)
    peers = members - 1
    for delta in [*range(-span, 0), *range(1, span + 1)]:
        present = (t + delta >= 0) & (t + delta < groups)
        peers = peers + present.astype(jnp.int32)

        @pl.when(present)
        def _(delta=delta):
            pl.semaphore_signal(
                barrier, inc=1, device_id={"tok": me + delta * members}, device_id_type=MESH_IDS
            )

    pl.semaphore_wait(barrier, peers)

    own = [
        pltpu.make_async_copy(pack_ref.at[g], weights_all.at[t, g], own_sems.at[0]),
        pltpu.make_async_copy(out_pack_ref.at[g], out_block_ref.at[g], own_sems.at[1]),
        pltpu.make_async_copy(normed_ref, rows_all.at[g], own_sems.at[2]),
        pltpu.make_async_copy(facts_ref, facts_window_ref.at[back, g], own_sems.at[3]),
    ]

    def fact_copy(step):
        j = lax.rem(g + step, members)
        return send(
            facts_ref, facts_window_ref.at[back, g], fact_send.at[step], fact_recv.at[step], base + j
        )

    def past_copy(distance):
        return send(
            facts_window_ref.at[back],
            facts_window_ref.at[back - distance],
            past_send.at[distance - 1],
            past_recv.at[distance - 1],
            me + distance * members,
        )


    def pack_copy(step):
        j = lax.rem(g + step, members)
        return send(
            pack_ref.at[j], weights_all.at[t, g], pack_send.at[step], pack_recv.at[step], base + j
        )

    def out_copy(step):
        j = lax.rem(g + step, members)
        return send(
            out_pack_ref.at[j], out_block_ref.at[g], out_send.at[step], out_recv.at[step], base + j
        )

    partner = base + g + 1 - 2 * lax.rem(g, 2)
    across_g = lax.rem(g + 2, members)
    across = base + across_g
    row_copies = [
        send(normed_ref, rows_all.at[g], row_send.at[0], row_recv.at[0], partner),
        send(normed_ref, rows_all.at[g], row_send.at[1], row_recv.at[1], across),
        send(rows_all.at[across_g], rows_all.at[across_g], row_send.at[2], row_recv.at[2], partner),
    ]
    for copy in own:
        copy.start()
    for step in range(1, members):
        fact_copy(step).start()
        pack_copy(step).start()
    row_copies[1].start()
    row_copies[0].start()
    for step in range(1, members):
        pack_copy(step).wait_recv()
    own[0].wait()

    def block_copy(block, way, device):
        return send(
            weights_all.at[block],
            weights_all.at[block],
            block_send.at[block, way],
            block_recv.at[block],
            device,
        )

    def forward(block, up, down):
        if up:

            @pl.when(z < depth_z - 1)
            def _():
                block_copy(block, 0, above).start()

        if down:

            @pl.when(z > 0)
            def _():
                block_copy(block, 1, below).start()

        block_copy(block, 2, side).start()

    def forward_done(block, up, down):
        if up:

            @pl.when(z < depth_z - 1)
            def _():
                block_copy(block, 0, above).wait_send()

        if down:

            @pl.when(z > 0)
            def _():
                block_copy(block, 1, below).wait_send()

        block_copy(block, 2, side).wait_send()

    forward(t, True, True)
    for step in range(1, members):
        out_copy(step).start()
        fact_copy(step).wait_recv()
    own[3].wait()
    for distance in range(1, back + 1):

        @pl.when(t + distance < groups)
        def _(distance=distance):
            past_copy(distance).start()

        @pl.when(t < distance)
        def _(distance=distance):
            facts_window_ref[back - distance] = jnp.full(
                facts_window_ref.shape[1:], -1, jnp.int32
            )

    row_copies[1].wait_recv()
    row_copies[2].start()
    for k in range(1, depth_z):

        @pl.when(z >= k)
        def _(k=k):
            block_copy(t - 2 * k, 0, above).wait_recv()
            forward(t - 2 * k, True, False)

        @pl.when(z + k < depth_z)
        def _(k=k):
            block_copy(t + 2 * k, 1, below).wait_recv()
            forward(t + 2 * k, False, True)

    row_copies[0].wait_recv()
    row_copies[2].wait_recv()
    own[1].wait()
    own[2].wait()
    for k in range(depth_z):
        block_copy(2 * k + 1 - y, 2, side).wait_recv()

    model = weights_all.shape[1] * weights_all.shape[2] * groups
    columns = weights_all.shape[3]
    query_cols = columns - 2 * HEAD_SIZE
    share = row_count
    width_k = model // groups

    def project(member, start, size):
        def add(block, total):
            piece = rows_all[member, :, pl.ds(pl.multiple_of(block * width_k, width_k), width_k)]
            weight = weights_all[block, :, :, pl.ds(start, size)].reshape(width_k, size)
            return total + jnp.dot(piece, weight, preferred_element_type=jnp.float32)

        total = jnp.zeros((row_count, size), jnp.float32)
        return lax.fori_loop(0, groups, add, total, unroll=True)

    @pl.loop(0, members)
    def _(member):
        rows = pl.ds(pl.multiple_of(member * share, share), share)
        both = project(member, query_cols, 2 * HEAD_SIZE)
        key = head_norm_rotate(
            both[:, :HEAD_SIZE], key_gain_ref[...], cos_ref[rows, :], sin_ref[rows, :]
        )
        kv_own[rows, :HEAD_SIZE] = key.astype(jnp.bfloat16)
        kv_own[rows, HEAD_SIZE:] = both[:, HEAD_SIZE:].astype(jnp.bfloat16)

    def slot(distance):
        full = window_rows - (distance + 1) * group_rows
        low = window_rows - group_rows - reach_rows
        skip = max(0, low - full)
        return skip, full + skip

    def kv_copy(distance):
        skip, start = slot(distance)
        return send(
            kv_own.at[pl.ds(skip, group_rows - skip)],
            window_ref.at[pl.ds(start, group_rows - skip)],
            kv_send.at[distance - 1],
            kv_recv.at[distance - 1],
            me + distance * members,
        )

    for distance in range(back, 0, -1):

        @pl.when(t + distance < groups)
        def _(distance=distance):
            kv_copy(distance).start()

        @pl.when(t < distance)
        def _(distance=distance):
            skip, start = slot(distance)
            window_ref[start : start + group_rows - skip, :] = jnp.zeros(
                (group_rows - skip, 2 * HEAD_SIZE), jnp.bfloat16
            )

    pad = window_rows - group_rows - reach_rows
    window_ref[:pad, :] = jnp.zeros((pad, 2 * HEAD_SIZE), jnp.bfloat16)

    pair = 2 * HEAD_SIZE

    @pl.loop(0, members)
    def _(member):
        rows = pl.ds(pl.multiple_of(member * share, share), share)
        window_ref[pl.ds(pl.multiple_of(window_rows - group_rows + member * share, 128), share), :] = kv_own[rows, :]

        @pl.loop(0, query_cols // pair)
        def _(h):
            both = project(member, pl.multiple_of(h * pair, pair), pair)
            for half in range(2):
                head = head_norm_rotate(
                    both[:, half * HEAD_SIZE : (half + 1) * HEAD_SIZE],
                    query_gain_ref[...],
                    cos_ref[rows, :],
                    sin_ref[rows, :],
                )
                query_ref[2 * h + half, rows, :] = head.astype(jnp.bfloat16)

    for distance in range(1, back + 1):

        @pl.when(t >= distance)
        def _(distance=distance):
            kv_copy(distance).wait_recv()
            past_copy(distance).wait_recv()

        @pl.when(t + distance < groups)
        def _(distance=distance):
            kv_copy(distance).wait_send()
            past_copy(distance).wait_send()

    for step in range(1, members):
        pack_copy(step).wait_send()
        fact_copy(step).wait_send()
        out_copy(step).wait()
    for copy in row_copies:
        copy.wait_send()
    forward_done(t, True, True)
    for k in range(1, depth_z):

        @pl.when(z >= k)
        def _(k=k):
            forward_done(t - 2 * k, True, False)

        @pl.when(z + k < depth_z)
        def _(k=k):
            forward_done(t + 2 * k, False, True)


def attention_kernel(counts, floors, query_ref, docs_ref, window_ref, tags_ref, out_ref, acc, peak, total):
    tile = pl.program_id(0)
    heads = query_ref.shape[0]
    window_rows = window_ref.shape[0]
    tiles = pl.num_programs(0)
    end = window_rows - (tiles - 1 - tile) * TILE_TOKENS
    factor = math.log2(math.e) / math.sqrt(HEAD_SIZE)
    query_at = end - TILE_TOKENS + lax.broadcasted_iota(jnp.int32, (CHUNK, TILE_TOKENS), 1)
    peak[...] = jnp.full_like(peak, MASKED)
    total[...] = jnp.zeros_like(total)
    acc[...] = jnp.zeros_like(acc)

    @pl.loop(0, counts[tile])
    def _(step):
        start = pl.multiple_of(end - (step + 1) * CHUNK, TILE_TOKENS)
        keys = window_ref[pl.ds(start, CHUNK), :HEAD_SIZE]
        values = window_ref[pl.ds(start, CHUNK), HEAD_SIZE:].T
        key_at = start + lax.broadcasted_iota(jnp.int32, (CHUNK, TILE_TOKENS), 0)
        tags = tags_ref[pl.ds(start, CHUNK), :]
        visible = (
            ((tags == docs_ref[...]) | (key_at == query_at))
            & (key_at <= query_at)
            & (key_at >= floors[tile])
        )
        bias = jnp.where(visible, 0.0, MASKED)
        bias = jnp.concatenate([bias, bias], axis=1)
        for pair in range(heads // 2):
            queries = query_ref[2 * pair : 2 * pair + 2].reshape(2 * TILE_TOKENS, HEAD_SIZE)
            scores = lax.dot_general(
                keys, queries, (((1,), (1,)), ((), ())), preferred_element_type=jnp.float32
            )
            scores = scores * factor + bias
            before = peak[pair]
            now = jnp.maximum(before, jnp.max(scores, axis=0, keepdims=True))
            shrink = jnp.exp2(before - now)
            weights = jnp.exp2(scores - now)
            total[pair] = total[pair] * shrink + jnp.sum(weights, axis=0, keepdims=True)
            acc[pair] = acc[pair] * shrink + jnp.dot(
                values, weights.astype(jnp.bfloat16), preferred_element_type=jnp.float32
            )
            peak[pair] = now

    for pair in range(heads // 2):
        mixed = (acc[pair] / total[pair]).T.astype(jnp.bfloat16)
        for half in range(2):
            columns = slice((2 * pair + half) * HEAD_SIZE, (2 * pair + half + 1) * HEAD_SIZE)
            out_ref[:, columns] = mixed[half * TILE_TOKENS : (half + 1) * TILE_TOKENS]


def output_kernel(
    members,
    groups,
    attended_ref,
    block_ref,
    out_ref,
    weights_all,
    sums,
    near_out,
    near_in,
    far_out,
    far_in,
    own_sem,
    block_send,
    block_recv,
    near_send,
    near_recv,
    far_send,
    far_recv,
):
    me = lax.axis_index("tok")
    g = lax.rem(me, members)
    t = lax.div(me, members)
    y = lax.rem(t, 2)
    z = lax.div(t, 2)
    depth_z = groups // 2
    base = me - g
    partner_g = g + 1 - 2 * lax.rem(g, 2)
    across_g = lax.rem(g + 2, members)
    diagonal_g = lax.rem(partner_g + 2, members)
    partner, across = base + partner_g, base + across_g
    side = me + members * (1 - 2 * y)
    below, above = me - 2 * members, me + 2 * members
    row_count = out_ref.shape[0]
    width = block_ref.shape[0]
    barrier = pltpu.get_barrier_semaphore()
    for other in (partner, across, side):
        pl.semaphore_signal(barrier, inc=1, device_id={"tok": other}, device_id_type=MESH_IDS)

    @pl.when(z > 0)
    def _():
        pl.semaphore_signal(barrier, inc=1, device_id={"tok": below}, device_id_type=MESH_IDS)

    @pl.when(z < depth_z - 1)
    def _():
        pl.semaphore_signal(barrier, inc=1, device_id={"tok": above}, device_id_type=MESH_IDS)

    own = pltpu.make_async_copy(block_ref, weights_all.at[t], own_sem)
    own.start()
    own.wait()
    pl.semaphore_wait(barrier, 3 + (z > 0).astype(jnp.int32) + (z < depth_z - 1).astype(jnp.int32))

    def block_copy(block, way, device):
        return send(
            weights_all.at[block],
            weights_all.at[block],
            block_send.at[block, way],
            block_recv.at[block],
            device,
        )

    near_z = jnp.minimum(z, depth_z - 1 - z)

    def plane(turn):
        step = lax.div(turn + 1, 2)
        both = z + step * (1 - 2 * lax.rem(turn, 2))
        rest = jnp.where(2 * z < depth_z - 1, turn, depth_z - 1 - turn)
        return jnp.where(turn <= 2 * near_z, both, rest)

    def block_at(turn):
        level = plane(lax.div(turn, 2))
        row = jnp.where(lax.rem(turn, 2) == 0, y, 1 - y)
        return level, 2 * level + row

    def partial(member, block):
        rows = pl.ds(pl.multiple_of(member * row_count, row_count), row_count)
        return lax.dot_general(
            attended_ref[rows, :],
            weights_all[block],
            (((1,), (1,)), ((), ())),
            preferred_element_type=jnp.float32,
        ).astype(jnp.bfloat16)

    def near(way, turn):
        return send(
            near_out.at[way, turn],
            near_in.at[way, turn],
            near_send.at[way, turn],
            near_recv.at[way, turn],
            partner,
        )

    def far(turn):
        return send(far_out.at[turn], far_in.at[turn], far_send.at[turn], far_recv.at[turn], across)

    @pl.loop(0, groups + 1)
    def _(turn):
        @pl.when(turn < groups)
        def _():
            level, block = block_at(turn)
            mine = lax.rem(turn, 2) == 0

            @pl.when(turn > 0)
            def _():
                block_copy(block, 2, side).wait_recv()

            @pl.when(mine & (level <= z) & (z < depth_z - 1))
            def _():
                block_copy(block, 0, above).start()

            @pl.when(mine & (level >= z) & (z > 0))
            def _():
                block_copy(block, 1, below).start()

            @pl.when(mine)
            def _():
                block_copy(block, 2, side).start()

            near_out[0, turn] = partial(diagonal_g, block)
            near(0, turn).start()
            near_out[1, turn] = partial(partner_g, block)
            near(1, turn).start()

        @pl.when(turn > 0)
        def _():
            past = turn - 1
            _, block = block_at(past)
            first = partial(across_g, block).astype(jnp.float32)
            near(0, past).wait_recv()
            far_out[past] = (first + near_in[0, past].astype(jnp.float32)).astype(jnp.bfloat16)
            far(past).start()
            second = partial(g, block).astype(jnp.float32)
            near(1, past).wait_recv()
            sums[past] = second + near_in[1, past].astype(jnp.float32)

    @pl.loop(0, groups)
    def _(turn):
        level, block = block_at(turn)
        mine = lax.rem(turn, 2) == 0
        far(turn).wait_recv()
        out_ref[:, pl.ds(pl.multiple_of(block * width, width), width)] = (
            sums[turn] + far_in[turn].astype(jnp.float32)
        ).astype(jnp.bfloat16)
        near(0, turn).wait_send()
        near(1, turn).wait_send()
        far(turn).wait_send()

        @pl.when(mine & (level <= z) & (z < depth_z - 1))
        def _():
            block_copy(block, 0, above).wait_send()

        @pl.when(mine & (level >= z) & (z > 0))
        def _():
            block_copy(block, 1, below).wait_send()

        @pl.when(mine)
        def _():
            block_copy(block, 2, side).wait_send()


VMEM_BYTES = 60 << 20


def in_vmem(count):
    return [pl.BlockSpec(memory_space=pltpu.VMEM)] * count


def grouped(
    tokens,
    norm_gain,
    w_query,
    key_weight,
    value_weight,
    query_gain,
    key_gain,
    w_out,
    doc_ids,
    sentinel,
    tile_reach,
):
    row_count = tokens.shape[0]
    depth = w_query.shape[0]
    members = key_weight.shape[1] // HEAD_SIZE
    devices = lax.axis_size("tok")
    groups = devices // members
    group_rows = members * row_count
    reach_rows = REACH_DEVS * row_count
    pad = CHUNK - TILE_TOKENS
    window_rows = pad + reach_rows + group_rows
    query_cols = w_query.shape[1] // members
    heads = query_cols // HEAD_SIZE
    model = tokens.shape[1]
    group = lax.axis_index("tok") // members
    base_row = group * group_rows

    lanes = HEAD_SIZE
    rows_each = row_count // lanes
    facts = jnp.concatenate(
        [
            doc_ids,
            sentinel,
            jnp.pad(tile_reach, (0, (8 - 2 * rows_each) * lanes - tile_reach.shape[0])),
        ]
    ).reshape(8, lanes)

    normed = rms_norm(tokens.astype(jnp.float32), norm_gain).astype(jnp.bfloat16)
    pack = jnp.concatenate(
        [
            w_query.reshape(depth, members, query_cols),
            key_weight.reshape(depth, members, HEAD_SIZE),
            value_weight.reshape(depth, members, HEAD_SIZE),
        ],
        axis=2,
    ).transpose(1, 0, 2)
    out_depth = w_out.shape[1]
    out_pack = w_out.T.reshape(out_depth, members, query_cols).transpose(1, 0, 2)
    positions = (base_row + jnp.arange(group_rows, dtype=jnp.int32)).astype(jnp.float32)
    half_width = HEAD_SIZE // 2
    freqs = THETA ** (-2.0 * jnp.arange(half_width, dtype=jnp.float32) / HEAD_SIZE)
    angles = positions[:, None] * freqs[None, :]
    cosine, sine = jnp.cos(angles), jnp.sin(angles)
    cosine = jnp.concatenate([cosine, cosine], axis=1)
    sine = jnp.concatenate([-sine, sine], axis=1)
    columns = query_cols + 2 * HEAD_SIZE
    back = -(-reach_rows // group_rows)
    dma = pltpu.SemaphoreType.DMA
    queries, window, out_block, facts_window = pl.pallas_call(
        functools.partial(project_kernel, members, groups, reach_rows),
        out_shape=(
            jax.ShapeDtypeStruct((heads, group_rows, HEAD_SIZE), jnp.bfloat16),
            jax.ShapeDtypeStruct((window_rows, 2 * HEAD_SIZE), jnp.bfloat16),
            jax.ShapeDtypeStruct((members, out_depth, query_cols), jnp.bfloat16),
            jax.ShapeDtypeStruct((back + 1, members, 8, lanes), jnp.int32),
        ),
        in_specs=in_vmem(8),
        out_specs=tuple(in_vmem(4)),
        scratch_shapes=[
            pltpu.VMEM((members, row_count, model), jnp.bfloat16),
            pltpu.VMEM((groups, members, depth, columns), jnp.bfloat16),
            pltpu.VMEM((group_rows, 2 * HEAD_SIZE), jnp.bfloat16),
            dma((4,)),
            dma((members,)),
            dma((members,)),
            dma((members,)),
            dma((members,)),
            dma((3,)),
            dma((3,)),
            dma((groups, 3)),
            dma((groups,)),
            dma((back,)),
            dma((back,)),
            dma((members,)),
            dma((members,)),
            dma((back,)),
            dma((back,)),
        ],
        compiler_params=pltpu.CompilerParams(
            collective_id=0, has_side_effects=True, vmem_limit_bytes=VMEM_BYTES
        ),
        name="project",
    )(normed, pack, out_pack, cosine, sine, query_gain[None, :], key_gain[None, :], facts)

    docs_all = facts_window[:, :, :rows_each].reshape(-1)[-window_rows:]
    sentinel_all = facts_window[:, :, rows_each : 2 * rows_each].reshape(-1)[-window_rows:]
    tags_window = jnp.where(sentinel_all == 1, 0, docs_all + 1)
    tags_window = jnp.broadcast_to(tags_window[:, None], (window_rows, TILE_TOKENS))
    tiles = group_rows // TILE_TOKENS
    query_docs = docs_all[-group_rows:]
    reach = facts_window[back, :, 2 * rows_each, : tile_reach.shape[0]].reshape(-1)
    first_row = window_rows - group_rows
    tile_start = first_row + jnp.arange(tiles, dtype=jnp.int32) * TILE_TOKENS
    first_doc = query_docs[::TILE_TOKENS]
    doc_start = jnp.sum((docs_all[None, :] < first_doc[:, None]).astype(jnp.int32), axis=1)
    floors = tile_start - reach * TILE_TOKENS
    lowest = jnp.maximum(floors, doc_start // TILE_TOKENS * TILE_TOKENS)
    counts = (tile_start + TILE_TOKENS - lowest + CHUNK - 1) // CHUNK

    attended = pl.pallas_call(
        attention_kernel,
        out_shape=jax.ShapeDtypeStruct((group_rows, query_cols), jnp.bfloat16),
        grid_spec=pltpu.PrefetchScalarGridSpec(
            num_scalar_prefetch=2,
            grid=(tiles,),
            in_specs=[
                pl.BlockSpec((heads, TILE_TOKENS, HEAD_SIZE), lambda i, *_: (0, i, 0)),
                pl.BlockSpec((1, TILE_TOKENS), lambda i, *_: (0, i)),
                pl.BlockSpec((window_rows, 2 * HEAD_SIZE), lambda i, *_: (0, 0)),
                pl.BlockSpec((window_rows, TILE_TOKENS), lambda i, *_: (0, 0)),
            ],
            out_specs=pl.BlockSpec((TILE_TOKENS, query_cols), lambda i, *_: (i, 0)),
            scratch_shapes=[
                pltpu.VMEM((heads // 2, HEAD_SIZE, 2 * TILE_TOKENS), jnp.float32),
                pltpu.VMEM((heads // 2, 1, 2 * TILE_TOKENS), jnp.float32),
                pltpu.VMEM((heads // 2, 1, 2 * TILE_TOKENS), jnp.float32),
            ],
        ),
        compiler_params=pltpu.CompilerParams(vmem_limit_bytes=VMEM_BYTES),
        cost_estimate=pl.CostEstimate(
            flops=2 * group_rows * window_rows * query_cols,
            bytes_accessed=window_rows * 4 * HEAD_SIZE + 4 * group_rows * query_cols,
            transcendentals=group_rows * window_rows * heads // 2,
        ),
        name="attend",
    )(counts, floors, queries, query_docs[None, :] + 1, window, tags_window)

    width = members * out_depth
    return pl.pallas_call(
        functools.partial(output_kernel, members, groups),
        out_shape=jax.ShapeDtypeStruct((row_count, model), jnp.bfloat16),
        in_specs=in_vmem(2),
        out_specs=in_vmem(1)[0],
        scratch_shapes=[
            pltpu.VMEM((groups, width, query_cols), jnp.bfloat16),
            pltpu.VMEM((groups, row_count, width), jnp.float32),
            pltpu.VMEM((2, groups, row_count, width), jnp.bfloat16),
            pltpu.VMEM((2, groups, row_count, width), jnp.bfloat16),
            pltpu.VMEM((groups, row_count, width), jnp.bfloat16),
            pltpu.VMEM((groups, row_count, width), jnp.bfloat16),
            dma,
            dma((groups, 3)),
            dma((groups,)),
            dma((2, groups)),
            dma((2, groups)),
            dma((groups,)),
            dma((groups,)),
        ],
        compiler_params=pltpu.CompilerParams(
            collective_id=1, has_side_effects=True, vmem_limit_bytes=VMEM_BYTES
        ),
        name="output",
    )(attended, out_block.reshape(width, query_cols))


def chosen(*arguments):
    members = arguments[3].shape[1] // HEAD_SIZE
    devices = lax.axis_size("tok")
    if lax.axis_size("head") == 1 and members == 4 and devices % (2 * members) == 0:
        return grouped(*arguments)
    return on_device(*arguments)


def solution(mesh):
    return jax.shard_map(
        chosen,
        mesh=mesh,
        in_specs=(
            P("tok", "head"),
            P(),
            P("tok", "head"),
            P("tok", "head"),
            P("tok", "head"),
            P(),
            P(),
            P("head", "tok"),
            P("tok"),
            P("tok"),
            P("tok"),
        ),
        out_specs=P("tok", "head"),
        check_vma=False,
    )
```

```python
import functools
import math

import jax
import jax.numpy as jnp
from jax import lax
from jax.experimental import pallas as pl
from jax.experimental.pallas import tpu as pltpu
from jax.sharding import PartitionSpec as P

HEAD_SIZE = 128
TILE_TOKENS = 128
REACH_DEVS = 14


EPSILON = 1e-06
THETA = 10000000.0


def passed_along(value, axis, steps):
    count = lax.axis_size(axis)
    leading, last = (max(0, -steps), min(count, count - steps))
    return lax.ppermute(value, axis, [(source, source + steps) for source in range(leading, last)])


def rms_norm(values, gain):
    mean_square = jnp.mean(values * values, axis=-1, keepdims=True)
    return values * lax.rsqrt(mean_square + EPSILON) * gain


def rotate(values, positions):
    width = values.shape[-1]
    half_width = width // 2
    freqs = THETA ** (-2.0 * jnp.arange(half_width, dtype=jnp.float32) / width)
    angles = positions[:, None] * freqs[None, :]
    cosine = jnp.cos(angles)[:, None, :]
    sine = jnp.sin(angles)[:, None, :]
    first = values[..., :half_width]
    second = values[..., half_width:]
    return jnp.concatenate(
        [first * cosine - second * sine, second * cosine + first * sine], axis=-1
    )


def on_device(
    tokens,
    norm_gain,
    w_query,
    key_weight,
    value_weight,
    query_gain,
    key_gain,
    w_out,
    doc_ids,
    sentinel,
    tile_reach,
):
    whole = lax.all_gather(tokens, "head", axis=1, tiled=True)
    row_count = whole.shape[0]
    normalized_rows = rms_norm(whole.astype(jnp.float32), norm_gain).astype(jnp.bfloat16)
    query_cols = w_query.shape[1]
    key_cols = key_weight.shape[1]
    portions = (
        lax.all_gather(w_query, "tok", axis=0, tiled=True),
        lax.all_gather(key_weight, "tok", axis=0, tiled=True),
        lax.all_gather(value_weight, "tok", axis=0, tiled=True),
    )
    proj_query, proj_key, proj_value = tuple(
        (
            jnp.dot(normalized_rows, portion, preferred_element_type=jnp.float32)
            for portion in portions
        )
    )
    base_row = lax.axis_index("tok") * row_count
    positions = (base_row + jnp.arange(row_count, dtype=jnp.int32)).astype(jnp.float32)
    local_heads = query_cols // HEAD_SIZE
    local_kv = key_cols // HEAD_SIZE
    head_groups = local_heads // local_kv
    query_matrix = rotate(
        rms_norm(proj_query.reshape(row_count, local_heads, HEAD_SIZE), query_gain), positions
    )
    query_matrix = query_matrix.astype(jnp.bfloat16).reshape(
        row_count, local_kv, head_groups, HEAD_SIZE
    )
    keys_own = rotate(
        rms_norm(proj_key.reshape(row_count, local_kv, HEAD_SIZE), key_gain), positions
    ).astype(jnp.bfloat16)
    values_own = proj_value.astype(jnp.bfloat16).reshape(row_count, local_kv, HEAD_SIZE)
    tags_own = jnp.where(sentinel == 1, 0, doc_ids + 1).astype(jnp.bfloat16)
    blocks = REACH_DEVS + 1

    def pass_along(step_index, state):
        current, key_store, value_store, tag_store = state
        current = passed_along((current[0], current[1], current[2]), "tok", 1)
        slot = REACH_DEVS - 1 - step_index
        key_store = lax.dynamic_update_index_in_dim(key_store, current[0], slot, 0)
        value_store = lax.dynamic_update_index_in_dim(value_store, current[1], slot, 0)
        tag_store = lax.dynamic_update_index_in_dim(tag_store, current[2], slot, 0)
        return (current, key_store, value_store, tag_store)

    key_store = (
        jnp.zeros((blocks, row_count, local_kv, HEAD_SIZE), jnp.bfloat16)
        .at[REACH_DEVS]
        .set(keys_own)
    )
    value_store = (
        jnp.zeros((blocks, row_count, local_kv, HEAD_SIZE), jnp.bfloat16)
        .at[REACH_DEVS]
        .set(values_own)
    )
    tag_store = jnp.zeros((blocks, row_count), jnp.bfloat16).at[REACH_DEVS].set(tags_own)
    state = lax.fori_loop(
        0,
        REACH_DEVS,
        pass_along,
        ((keys_own, values_own, tags_own), key_store, value_store, tag_store),
    )
    key_store, value_store, tag_store = (state[1], state[2], state[3])
    factor_scale = 1.0 / math.sqrt(HEAD_SIZE)
    outputs = []
    for tile_index in range(row_count // TILE_TOKENS):
        query_tile = query_matrix[tile_index * TILE_TOKENS : (tile_index + 1) * TILE_TOKENS]
        query_pos = base_row + tile_index * TILE_TOKENS + jnp.arange(TILE_TOKENS, dtype=jnp.int32)
        query_docs = doc_ids[tile_index * TILE_TOKENS : (tile_index + 1) * TILE_TOKENS] + 1
        lowest = base_row // TILE_TOKENS + tile_index - tile_reach[tile_index]

        def update(
            block,
            state,
            query_tile=query_tile,
            query_pos=query_pos,
            query_docs=query_docs,
            lowest=lowest,
        ):
            key_block = key_store[block]
            value_block = value_store[block]
            tag_block = tag_store[block].astype(jnp.int32)
            key_pos = (
                base_row + (block - REACH_DEVS) * row_count + jnp.arange(row_count, dtype=jnp.int32)
            )
            same_doc = (tag_block[None, :] == query_docs[:, None]) | (
                key_pos[None, :] == query_pos[:, None]
            )
            visible = (
                same_doc
                & (key_pos[None, :] <= query_pos[:, None])
                & (jnp.floor_divide(key_pos, TILE_TOKENS)[None, :] >= lowest)
            )

            def compute(inner):
                peak_run, weight_sum, accum_out = inner
                scores = (
                    jnp.einsum(
                        "qcgd,kcd->cgqk", query_tile, key_block, preferred_element_type=jnp.float32
                    )
                    * factor_scale
                )
                scores = jnp.where(visible, scores, -jnp.inf)
                peak_new = jnp.maximum(peak_run, jnp.max(scores, axis=-1))
                shrink = jnp.exp(peak_run - peak_new)
                weights = jnp.exp(scores - peak_new[..., None])
                weight_sum = weight_sum * shrink + jnp.sum(weights, axis=-1)
                mixed = jnp.einsum(
                    "cgqk,kcd->cgqd",
                    weights.astype(jnp.bfloat16),
                    value_block,
                    preferred_element_type=jnp.float32,
                )
                return (peak_new, weight_sum, accum_out * shrink[..., None] + mixed)

            return lax.cond(jnp.any(visible), compute, lambda inner: inner, state)

        initial = (
            jnp.full((local_kv, head_groups, TILE_TOKENS), -1e30, jnp.float32),
            jnp.zeros((local_kv, head_groups, TILE_TOKENS), jnp.float32),
            jnp.zeros((local_kv, head_groups, TILE_TOKENS, HEAD_SIZE), jnp.float32),
        )
        peak_run, weight_sum, accum_out = lax.fori_loop(0, blocks, update, initial)
        result = accum_out / weight_sum[..., None]
        outputs.append(
            jnp.transpose(result, (2, 0, 1, 3))
            .reshape(TILE_TOKENS, query_cols)
            .astype(jnp.bfloat16)
        )
    attended = jnp.concatenate(outputs, axis=0)
    partials = jnp.dot(
        attended,
        lax.all_gather(w_out, "tok", axis=1, tiled=True),
        preferred_element_type=jnp.float32,
    )
    return lax.psum_scatter(partials.astype(jnp.bfloat16), "head", scatter_dimension=1, tiled=True)


CHUNK = 512
MESH_IDS = pl.DeviceIdType.MESH
MASKED = -1e30


def send(source, target, send_sem, recv_sem, device):
    return pltpu.make_async_remote_copy(
        src_ref=source,
        dst_ref=target,
        send_sem=send_sem,
        recv_sem=recv_sem,
        device_id={"tok": device},
        device_id_type=MESH_IDS,
    )


def head_norm_rotate(values, gain, cosine, sine):
    mean_square = jnp.mean(values * values, axis=-1, keepdims=True)
    normed = values * lax.rsqrt(mean_square + EPSILON) * gain
    return normed * cosine + pltpu.roll(normed, HEAD_SIZE // 2, 1) * sine


def project_kernel(
    members,
    groups,
    reach_rows,
    normed_ref,
    pack_ref,
    out_pack_ref,
    cos_ref,
    sin_ref,
    query_gain_ref,
    key_gain_ref,
    facts_ref,
    query_ref,
    window_ref,
    out_block_ref,
    facts_window_ref,
    rows_all,
    weights_all,
    kv_own,
    own_sems,
    pack_send,
    pack_recv,
    out_send,
    out_recv,
    row_send,
    row_recv,
    block_send,
    block_recv,
    kv_send,
    kv_recv,
    fact_send,
    fact_recv,
    past_send,
    past_recv,
):
    me = lax.axis_index("tok")
    g = lax.rem(me, members)
    t = lax.div(me, members)
    y = lax.rem(t, 2)
    z = lax.div(t, 2)
    depth_z = groups // 2
    base = t * members
    side = me + members * (1 - 2 * y)
    below, above = me - 2 * members, me + 2 * members
    row_count = normed_ref.shape[0]
    group_rows = members * row_count
    back = -(-reach_rows // group_rows)
    window_rows = window_ref.shape[0]

    barrier = pltpu.get_barrier_semaphore()
    for step in range(1, members):
        other = base + lax.rem(g + step, members)
        pl.semaphore_signal(barrier, inc=1, device_id={"tok": other}, device_id_type=MESH_IDS)
    span = max(back, 2)
    peers = members - 1
    for delta in [*range(-span, 0), *range(1, span + 1)]:
        present = (t + delta >= 0) & (t + delta < groups)
        peers = peers + present.astype(jnp.int32)

        @pl.when(present)
        def _(delta=delta):
            pl.semaphore_signal(
                barrier, inc=1, device_id={"tok": me + delta * members}, device_id_type=MESH_IDS
            )

    pl.semaphore_wait(barrier, peers)

    own = [
        pltpu.make_async_copy(pack_ref.at[g], weights_all.at[t, g], own_sems.at[0]),
        pltpu.make_async_copy(out_pack_ref.at[g], out_block_ref.at[g], own_sems.at[1]),
        pltpu.make_async_copy(normed_ref, rows_all.at[g], own_sems.at[2]),
        pltpu.make_async_copy(facts_ref, facts_window_ref.at[back, g], own_sems.at[3]),
    ]

    def fact_copy(step):
        j = lax.rem(g + step, members)
        return send(
            facts_ref, facts_window_ref.at[back, g], fact_send.at[step], fact_recv.at[step], base + j
        )

    def past_copy(distance):
        return send(
            facts_window_ref.at[back],
            facts_window_ref.at[back - distance],
            past_send.at[distance - 1],
            past_recv.at[distance - 1],
            me + distance * members,
        )


    def pack_copy(step):
        j = lax.rem(g + step, members)
        return send(
            pack_ref.at[j], weights_all.at[t, g], pack_send.at[step], pack_recv.at[step], base + j
        )

    def out_copy(step):
        j = lax.rem(g + step, members)
        return send(
            out_pack_ref.at[j], out_block_ref.at[g], out_send.at[step], out_recv.at[step], base + j
        )

    partner = base + g + 1 - 2 * lax.rem(g, 2)
    across_g = lax.rem(g + 2, members)
    across = base + across_g
    row_copies = [
        send(normed_ref, rows_all.at[g], row_send.at[0], row_recv.at[0], partner),
        send(normed_ref, rows_all.at[g], row_send.at[1], row_recv.at[1], across),
        send(rows_all.at[across_g], rows_all.at[across_g], row_send.at[2], row_recv.at[2], partner),
    ]
    for copy in own:
        copy.start()
    for step in range(1, members):
        fact_copy(step).start()
        pack_copy(step).start()
    row_copies[1].start()
    row_copies[0].start()
    for step in range(1, members):
        pack_copy(step).wait_recv()
    own[0].wait()

    def block_copy(block, way, device):
        return send(
            weights_all.at[block],
            weights_all.at[block],
            block_send.at[block, way],
            block_recv.at[block],
            device,
        )

    def forward(block, up, down):
        if up:

            @pl.when(z < depth_z - 1)
            def _():
                block_copy(block, 0, above).start()

        if down:

            @pl.when(z > 0)
            def _():
                block_copy(block, 1, below).start()

        block_copy(block, 2, side).start()

    def forward_done(block, up, down):
        if up:

            @pl.when(z < depth_z - 1)
            def _():
                block_copy(block, 0, above).wait_send()

        if down:

            @pl.when(z > 0)
            def _():
                block_copy(block, 1, below).wait_send()

        block_copy(block, 2, side).wait_send()

    forward(t, True, True)
    for step in range(1, members):
        out_copy(step).start()
        fact_copy(step).wait_recv()
    own[3].wait()
    for distance in range(1, back + 1):

        @pl.when(t + distance < groups)
        def _(distance=distance):
            past_copy(distance).start()

        @pl.when(t < distance)
        def _(distance=distance):
            facts_window_ref[back - distance] = jnp.full(
                facts_window_ref.shape[1:], -1, jnp.int32
            )

    row_copies[1].wait_recv()
    row_copies[2].start()
    for k in range(1, depth_z):

        @pl.when(z >= k)
        def _(k=k):
            block_copy(t - 2 * k, 0, above).wait_recv()
            forward(t - 2 * k, True, False)

        @pl.when(z + k < depth_z)
        def _(k=k):
            block_copy(t + 2 * k, 1, below).wait_recv()
            forward(t + 2 * k, False, True)

    row_copies[0].wait_recv()
    row_copies[2].wait_recv()
    own[1].wait()
    own[2].wait()
    for k in range(depth_z):
        block_copy(2 * k + 1 - y, 2, side).wait_recv()

    model = weights_all.shape[1] * weights_all.shape[2] * groups
    columns = weights_all.shape[3]
    query_cols = columns - 2 * HEAD_SIZE
    share = row_count
    width_k = model // groups

    def project(member, start, size):
        def add(block, total):
            piece = rows_all[member, :, pl.ds(pl.multiple_of(block * width_k, width_k), width_k)]
            weight = weights_all[block, :, :, pl.ds(start, size)].reshape(width_k, size)
            return total + jnp.dot(piece, weight, preferred_element_type=jnp.float32)

        total = jnp.zeros((row_count, size), jnp.float32)
        return lax.fori_loop(0, groups, add, total, unroll=True)

    @pl.loop(0, members)
    def _(member):
        rows = pl.ds(pl.multiple_of(member * share, share), share)
        both = project(member, query_cols, 2 * HEAD_SIZE)
        key = head_norm_rotate(
            both[:, :HEAD_SIZE], key_gain_ref[...], cos_ref[rows, :], sin_ref[rows, :]
        )
        kv_own[rows, :HEAD_SIZE] = key.astype(jnp.bfloat16)
        kv_own[rows, HEAD_SIZE:] = both[:, HEAD_SIZE:].astype(jnp.bfloat16)

    def slot(distance):
        full = window_rows - (distance + 1) * group_rows
        low = window_rows - group_rows - reach_rows
        skip = max(0, low - full)
        return skip, full + skip

    def slot_ref(distance, skipped=0):
        skip, start = slot(distance)
        drop = max(skipped - skip, 0)
        return window_ref.at[pl.ds(start + drop, group_rows - skip - drop)]

    far_skip = slot(4)[0]

    def kv_copy(source, distance, way, device):
        return send(
            source, slot_ref(distance), kv_send.at[way], kv_recv.at[distance - 1], device
        )

    own_up = kv_copy(kv_own, 2, 0, above)
    own_side = kv_copy(kv_own, 1, 1, side)
    second_side_low = kv_copy(slot_ref(2), 3, 2, side)
    second_side_high = kv_copy(slot_ref(2), 1, 2, side)
    second_up = kv_copy(slot_ref(2, far_skip), 4, 3, above)
    first_up = kv_copy(slot_ref(1), 3, 4, above)
    has_above = z < depth_z - 1

    def kv_wait(distance):
        kv_copy(slot_ref(distance), distance, 0, side).wait_recv()

    @pl.when(has_above)
    def _():
        own_up.start()

    @pl.when(y == 0)
    def _():
        own_side.start()

    for distance in range(back, 0, -1):

        @pl.when(t < distance)
        def _(distance=distance):
            skip, start = slot(distance)
            window_ref[start : start + group_rows - skip, :] = jnp.zeros(
                (group_rows - skip, 2 * HEAD_SIZE), jnp.bfloat16
            )

    pad = window_rows - group_rows - reach_rows
    window_ref[:pad, :] = jnp.zeros((pad, 2 * HEAD_SIZE), jnp.bfloat16)

    pair = 2 * HEAD_SIZE

    def project_queries(first, last):
        @pl.loop(first, last)
        def _(member):
            rows = pl.ds(pl.multiple_of(member * share, share), share)
            place = pl.multiple_of(window_rows - group_rows + member * share, 128)
            window_ref[pl.ds(place, share), :] = kv_own[rows, :]

            @pl.loop(0, query_cols // pair)
            def _(h):
                both = project(member, pl.multiple_of(h * pair, pair), pair)
                for half in range(2):
                    head = head_norm_rotate(
                        both[:, half * HEAD_SIZE : (half + 1) * HEAD_SIZE],
                        query_gain_ref[...],
                        cos_ref[rows, :],
                        sin_ref[rows, :],
                    )
                    query_ref[2 * h + half, rows, :] = head.astype(jnp.bfloat16)

    project_queries(0, members // 2)

    @pl.when(z >= 1)
    def _():
        kv_wait(2)

        @pl.when(has_above)
        def _():
            second_up.start()

        @pl.when(y == 0)
        def _():
            second_side_low.start()

        @pl.when(y == 1)
        def _():
            second_side_high.start()

    project_queries(members // 2, members)

    @pl.when((y == 0) & (z >= 1))
    def _():
        kv_wait(1)

        @pl.when(has_above)
        def _():
            first_up.start()

    @pl.when(y == 1)
    def _():
        kv_wait(1)

    for distance in (3, 4):

        @pl.when(t >= distance)
        def _(distance=distance):
            kv_wait(distance)

    @pl.when(has_above)
    def _():
        own_up.wait_send()

        @pl.when(z >= 1)
        def _():
            second_up.wait_send()

    @pl.when(y == 0)
    def _():
        own_side.wait_send()

    @pl.when(z >= 1)
    def _():
        @pl.when(y == 0)
        def _():
            second_side_low.wait_send()

            @pl.when(has_above)
            def _():
                first_up.wait_send()

        @pl.when(y == 1)
        def _():
            second_side_high.wait_send()

    for distance in range(1, back + 1):

        @pl.when(t >= distance)
        def _(distance=distance):
            past_copy(distance).wait_recv()

        @pl.when(t + distance < groups)
        def _(distance=distance):
            past_copy(distance).wait_send()

    for step in range(1, members):
        pack_copy(step).wait_send()
        fact_copy(step).wait_send()
        out_copy(step).wait()
    for copy in row_copies:
        copy.wait_send()
    forward_done(t, True, True)
    for k in range(1, depth_z):

        @pl.when(z >= k)
        def _(k=k):
            forward_done(t - 2 * k, True, False)

        @pl.when(z + k < depth_z)
        def _(k=k):
            forward_done(t + 2 * k, False, True)


def attention_kernel(counts, floors, query_ref, docs_ref, window_ref, tags_ref, out_ref, acc, peak, total):
    tile = pl.program_id(0)
    heads = query_ref.shape[0]
    window_rows = window_ref.shape[0]
    tiles = pl.num_programs(0)
    end = window_rows - (tiles - 1 - tile) * TILE_TOKENS
    factor = math.log2(math.e) / math.sqrt(HEAD_SIZE)
    query_at = end - TILE_TOKENS + lax.broadcasted_iota(jnp.int32, (CHUNK, TILE_TOKENS), 1)
    peak[...] = jnp.full_like(peak, MASKED)
    total[...] = jnp.zeros_like(total)
    acc[...] = jnp.zeros_like(acc)

    @pl.loop(0, counts[tile])
    def _(step):
        start = pl.multiple_of(end - (step + 1) * CHUNK, TILE_TOKENS)
        keys = window_ref[pl.ds(start, CHUNK), :HEAD_SIZE]
        values = window_ref[pl.ds(start, CHUNK), HEAD_SIZE:].T
        key_at = start + lax.broadcasted_iota(jnp.int32, (CHUNK, TILE_TOKENS), 0)
        tags = tags_ref[pl.ds(start, CHUNK), :]
        visible = (
            ((tags == docs_ref[...]) | (key_at == query_at))
            & (key_at <= query_at)
            & (key_at >= floors[tile])
        )
        bias = jnp.where(visible, 0.0, MASKED)
        bias = jnp.concatenate([bias, bias], axis=1)
        for pair in range(heads // 2):
            queries = query_ref[2 * pair : 2 * pair + 2].reshape(2 * TILE_TOKENS, HEAD_SIZE)
            scores = lax.dot_general(
                keys, queries, (((1,), (1,)), ((), ())), preferred_element_type=jnp.float32
            )
            scores = scores * factor + bias
            before = peak[pair]
            now = jnp.maximum(before, jnp.max(scores, axis=0, keepdims=True))
            shrink = jnp.exp2(before - now)
            weights = jnp.exp2(scores - now)
            total[pair] = total[pair] * shrink + jnp.sum(weights, axis=0, keepdims=True)
            acc[pair] = acc[pair] * shrink + jnp.dot(
                values, weights.astype(jnp.bfloat16), preferred_element_type=jnp.float32
            )
            peak[pair] = now

    for pair in range(heads // 2):
        mixed = (acc[pair] / total[pair]).T.astype(jnp.bfloat16)
        for half in range(2):
            columns = slice((2 * pair + half) * HEAD_SIZE, (2 * pair + half + 1) * HEAD_SIZE)
            out_ref[:, columns] = mixed[half * TILE_TOKENS : (half + 1) * TILE_TOKENS]


def output_kernel(
    members,
    groups,
    attended_ref,
    block_ref,
    out_ref,
    weights_all,
    sums,
    near_out,
    near_in,
    far_out,
    far_in,
    own_sem,
    block_send,
    block_recv,
    near_send,
    near_recv,
    far_send,
    far_recv,
):
    me = lax.axis_index("tok")
    g = lax.rem(me, members)
    t = lax.div(me, members)
    y = lax.rem(t, 2)
    z = lax.div(t, 2)
    depth_z = groups // 2
    base = me - g
    partner_g = g + 1 - 2 * lax.rem(g, 2)
    across_g = lax.rem(g + 2, members)
    diagonal_g = lax.rem(partner_g + 2, members)
    partner, across = base + partner_g, base + across_g
    side = me + members * (1 - 2 * y)
    below, above = me - 2 * members, me + 2 * members
    row_count = out_ref.shape[0]
    width = block_ref.shape[0]
    barrier = pltpu.get_barrier_semaphore()
    for other in (partner, across, side):
        pl.semaphore_signal(barrier, inc=1, device_id={"tok": other}, device_id_type=MESH_IDS)

    @pl.when(z > 0)
    def _():
        pl.semaphore_signal(barrier, inc=1, device_id={"tok": below}, device_id_type=MESH_IDS)

    @pl.when(z < depth_z - 1)
    def _():
        pl.semaphore_signal(barrier, inc=1, device_id={"tok": above}, device_id_type=MESH_IDS)

    own = pltpu.make_async_copy(block_ref, weights_all.at[t], own_sem)
    own.start()
    own.wait()
    pl.semaphore_wait(barrier, 3 + (z > 0).astype(jnp.int32) + (z < depth_z - 1).astype(jnp.int32))

    def block_copy(block, way, device):
        return send(
            weights_all.at[block],
            weights_all.at[block],
            block_send.at[block, way],
            block_recv.at[block],
            device,
        )

    near_z = jnp.minimum(z, depth_z - 1 - z)

    def plane(turn):
        step = lax.div(turn + 1, 2)
        both = z + step * (1 - 2 * lax.rem(turn, 2))
        rest = jnp.where(2 * z < depth_z - 1, turn, depth_z - 1 - turn)
        return jnp.where(turn <= 2 * near_z, both, rest)

    def block_at(turn):
        level = plane(lax.div(turn, 2))
        row = jnp.where(lax.rem(turn, 2) == 0, y, 1 - y)
        return level, 2 * level + row

    def partial(member, block):
        rows = pl.ds(pl.multiple_of(member * row_count, row_count), row_count)
        return lax.dot_general(
            attended_ref[rows, :],
            weights_all[block],
            (((1,), (1,)), ((), ())),
            preferred_element_type=jnp.float32,
        ).astype(jnp.bfloat16)

    def near(way, turn):
        return send(
            near_out.at[way, turn],
            near_in.at[way, turn],
            near_send.at[way, turn],
            near_recv.at[way, turn],
            partner,
        )

    def far(turn):
        return send(far_out.at[turn], far_in.at[turn], far_send.at[turn], far_recv.at[turn], across)

    @pl.loop(0, groups + 1)
    def _(turn):
        @pl.when(turn < groups)
        def _():
            level, block = block_at(turn)
            mine = lax.rem(turn, 2) == 0

            @pl.when(turn > 0)
            def _():
                block_copy(block, 2, side).wait_recv()

            @pl.when(mine & (level <= z) & (z < depth_z - 1))
            def _():
                block_copy(block, 0, above).start()

            @pl.when(mine & (level >= z) & (z > 0))
            def _():
                block_copy(block, 1, below).start()

            @pl.when(mine)
            def _():
                block_copy(block, 2, side).start()

            near_out[0, turn] = partial(diagonal_g, block)
            near(0, turn).start()
            near_out[1, turn] = partial(partner_g, block)
            near(1, turn).start()

        @pl.when(turn > 0)
        def _():
            past = turn - 1
            _, block = block_at(past)
            first = partial(across_g, block).astype(jnp.float32)
            near(0, past).wait_recv()
            far_out[past] = (first + near_in[0, past].astype(jnp.float32)).astype(jnp.bfloat16)
            far(past).start()
            second = partial(g, block).astype(jnp.float32)
            near(1, past).wait_recv()
            sums[past] = second + near_in[1, past].astype(jnp.float32)

    @pl.loop(0, groups)
    def _(turn):
        level, block = block_at(turn)
        mine = lax.rem(turn, 2) == 0
        far(turn).wait_recv()
        out_ref[:, pl.ds(pl.multiple_of(block * width, width), width)] = (
            sums[turn] + far_in[turn].astype(jnp.float32)
        ).astype(jnp.bfloat16)
        near(0, turn).wait_send()
        near(1, turn).wait_send()
        far(turn).wait_send()

        @pl.when(mine & (level <= z) & (z < depth_z - 1))
        def _():
            block_copy(block, 0, above).wait_send()

        @pl.when(mine & (level >= z) & (z > 0))
        def _():
            block_copy(block, 1, below).wait_send()

        @pl.when(mine)
        def _():
            block_copy(block, 2, side).wait_send()


VMEM_BYTES = 60 << 20


def in_vmem(count):
    return [pl.BlockSpec(memory_space=pltpu.VMEM)] * count


def grouped(
    tokens,
    norm_gain,
    w_query,
    key_weight,
    value_weight,
    query_gain,
    key_gain,
    w_out,
    doc_ids,
    sentinel,
    tile_reach,
):
    row_count = tokens.shape[0]
    depth = w_query.shape[0]
    members = key_weight.shape[1] // HEAD_SIZE
    devices = lax.axis_size("tok")
    groups = devices // members
    group_rows = members * row_count
    reach_rows = REACH_DEVS * row_count
    pad = CHUNK - TILE_TOKENS
    window_rows = pad + reach_rows + group_rows
    query_cols = w_query.shape[1] // members
    heads = query_cols // HEAD_SIZE
    model = tokens.shape[1]
    group = lax.axis_index("tok") // members
    base_row = group * group_rows

    lanes = HEAD_SIZE
    rows_each = row_count // lanes
    facts = jnp.concatenate(
        [
            doc_ids,
            sentinel,
            jnp.pad(tile_reach, (0, (8 - 2 * rows_each) * lanes - tile_reach.shape[0])),
        ]
    ).reshape(8, lanes)

    normed = rms_norm(tokens.astype(jnp.float32), norm_gain).astype(jnp.bfloat16)
    pack = jnp.concatenate(
        [
            w_query.reshape(depth, members, query_cols),
            key_weight.reshape(depth, members, HEAD_SIZE),
            value_weight.reshape(depth, members, HEAD_SIZE),
        ],
        axis=2,
    ).transpose(1, 0, 2)
    out_depth = w_out.shape[1]
    out_pack = w_out.T.reshape(out_depth, members, query_cols).transpose(1, 0, 2)
    positions = (base_row + jnp.arange(group_rows, dtype=jnp.int32)).astype(jnp.float32)
    half_width = HEAD_SIZE // 2
    freqs = THETA ** (-2.0 * jnp.arange(half_width, dtype=jnp.float32) / HEAD_SIZE)
    angles = positions[:, None] * freqs[None, :]
    cosine, sine = jnp.cos(angles), jnp.sin(angles)
    cosine = jnp.concatenate([cosine, cosine], axis=1)
    sine = jnp.concatenate([-sine, sine], axis=1)
    columns = query_cols + 2 * HEAD_SIZE
    back = -(-reach_rows // group_rows)
    dma = pltpu.SemaphoreType.DMA
    queries, window, out_block, facts_window = pl.pallas_call(
        functools.partial(project_kernel, members, groups, reach_rows),
        out_shape=(
            jax.ShapeDtypeStruct((heads, group_rows, HEAD_SIZE), jnp.bfloat16),
            jax.ShapeDtypeStruct((window_rows, 2 * HEAD_SIZE), jnp.bfloat16),
            jax.ShapeDtypeStruct((members, out_depth, query_cols), jnp.bfloat16),
            jax.ShapeDtypeStruct((back + 1, members, 8, lanes), jnp.int32),
        ),
        in_specs=in_vmem(8),
        out_specs=tuple(in_vmem(4)),
        scratch_shapes=[
            pltpu.VMEM((members, row_count, model), jnp.bfloat16),
            pltpu.VMEM((groups, members, depth, columns), jnp.bfloat16),
            pltpu.VMEM((group_rows, 2 * HEAD_SIZE), jnp.bfloat16),
            dma((4,)),
            dma((members,)),
            dma((members,)),
            dma((members,)),
            dma((members,)),
            dma((3,)),
            dma((3,)),
            dma((groups, 3)),
            dma((groups,)),
            dma((5,)),
            dma((back,)),
            dma((members,)),
            dma((members,)),
            dma((back,)),
            dma((back,)),
        ],
        compiler_params=pltpu.CompilerParams(
            collective_id=0, has_side_effects=True, vmem_limit_bytes=VMEM_BYTES
        ),
        name="project",
    )(normed, pack, out_pack, cosine, sine, query_gain[None, :], key_gain[None, :], facts)

    docs_all = facts_window[:, :, :rows_each].reshape(-1)[-window_rows:]
    sentinel_all = facts_window[:, :, rows_each : 2 * rows_each].reshape(-1)[-window_rows:]
    tags_window = jnp.where(sentinel_all == 1, 0, docs_all + 1)
    tags_window = jnp.broadcast_to(tags_window[:, None], (window_rows, TILE_TOKENS))
    tiles = group_rows // TILE_TOKENS
    query_docs = docs_all[-group_rows:]
    reach = facts_window[back, :, 2 * rows_each, : tile_reach.shape[0]].reshape(-1)
    first_row = window_rows - group_rows
    tile_start = first_row + jnp.arange(tiles, dtype=jnp.int32) * TILE_TOKENS
    first_doc = query_docs[::TILE_TOKENS]
    doc_start = jnp.sum((docs_all[None, :] < first_doc[:, None]).astype(jnp.int32), axis=1)
    floors = tile_start - reach * TILE_TOKENS
    lowest = jnp.maximum(floors, doc_start // TILE_TOKENS * TILE_TOKENS)
    counts = (tile_start + TILE_TOKENS - lowest + CHUNK - 1) // CHUNK

    attended = pl.pallas_call(
        attention_kernel,
        out_shape=jax.ShapeDtypeStruct((group_rows, query_cols), jnp.bfloat16),
        grid_spec=pltpu.PrefetchScalarGridSpec(
            num_scalar_prefetch=2,
            grid=(tiles,),
            in_specs=[
                pl.BlockSpec((heads, TILE_TOKENS, HEAD_SIZE), lambda i, *_: (0, i, 0)),
                pl.BlockSpec((1, TILE_TOKENS), lambda i, *_: (0, i)),
                pl.BlockSpec((window_rows, 2 * HEAD_SIZE), lambda i, *_: (0, 0)),
                pl.BlockSpec((window_rows, TILE_TOKENS), lambda i, *_: (0, 0)),
            ],
            out_specs=pl.BlockSpec((TILE_TOKENS, query_cols), lambda i, *_: (i, 0)),
            scratch_shapes=[
                pltpu.VMEM((heads // 2, HEAD_SIZE, 2 * TILE_TOKENS), jnp.float32),
                pltpu.VMEM((heads // 2, 1, 2 * TILE_TOKENS), jnp.float32),
                pltpu.VMEM((heads // 2, 1, 2 * TILE_TOKENS), jnp.float32),
            ],
        ),
        compiler_params=pltpu.CompilerParams(vmem_limit_bytes=VMEM_BYTES),
        cost_estimate=pl.CostEstimate(
            flops=2 * group_rows * window_rows * query_cols,
            bytes_accessed=window_rows * 4 * HEAD_SIZE + 4 * group_rows * query_cols,
            transcendentals=group_rows * window_rows * heads // 2,
        ),
        name="attend",
    )(counts, floors, queries, query_docs[None, :] + 1, window, tags_window)

    width = members * out_depth
    return pl.pallas_call(
        functools.partial(output_kernel, members, groups),
        out_shape=jax.ShapeDtypeStruct((row_count, model), jnp.bfloat16),
        in_specs=in_vmem(2),
        out_specs=in_vmem(1)[0],
        scratch_shapes=[
            pltpu.VMEM((groups, width, query_cols), jnp.bfloat16),
            pltpu.VMEM((groups, row_count, width), jnp.float32),
            pltpu.VMEM((2, groups, row_count, width), jnp.bfloat16),
            pltpu.VMEM((2, groups, row_count, width), jnp.bfloat16),
            pltpu.VMEM((groups, row_count, width), jnp.bfloat16),
            pltpu.VMEM((groups, row_count, width), jnp.bfloat16),
            dma,
            dma((groups, 3)),
            dma((groups,)),
            dma((2, groups)),
            dma((2, groups)),
            dma((groups,)),
            dma((groups,)),
        ],
        compiler_params=pltpu.CompilerParams(
            collective_id=1, has_side_effects=True, vmem_limit_bytes=VMEM_BYTES
        ),
        name="output",
    )(attended, out_block.reshape(width, query_cols))


def chosen(*arguments):
    members = arguments[3].shape[1] // HEAD_SIZE
    devices = lax.axis_size("tok")
    near_enough = 3 * members < REACH_DEVS <= 4 * members
    if lax.axis_size("head") == 1 and members == 4 and near_enough and devices % 8 == 0:
        return grouped(*arguments)
    return on_device(*arguments)


def solution(mesh):
    return jax.shard_map(
        chosen,
        mesh=mesh,
        in_specs=(
            P("tok", "head"),
            P(),
            P("tok", "head"),
            P("tok", "head"),
            P("tok", "head"),
            P(),
            P(),
            P("head", "tok"),
            P("tok"),
            P("tok"),
            P("tok"),
        ),
        out_specs=P("tok", "head"),
        check_vma=False,
    )
```

```python
import functools
import math

import jax
import jax.numpy as jnp
from jax import lax
from jax.experimental import pallas as pl
from jax.experimental.pallas import tpu as pltpu
from jax.sharding import PartitionSpec as P

HEAD_SIZE = 128
TILE_TOKENS = 128
REACH_DEVS = 14


EPSILON = 1e-06
THETA = 10000000.0


def passed_along(value, axis, steps):
    count = lax.axis_size(axis)
    leading, last = (max(0, -steps), min(count, count - steps))
    return lax.ppermute(value, axis, [(source, source + steps) for source in range(leading, last)])


def rms_norm(values, gain):
    mean_square = jnp.mean(values * values, axis=-1, keepdims=True)
    return values * lax.rsqrt(mean_square + EPSILON) * gain


def rotate(values, positions):
    width = values.shape[-1]
    half_width = width // 2
    freqs = THETA ** (-2.0 * jnp.arange(half_width, dtype=jnp.float32) / width)
    angles = positions[:, None] * freqs[None, :]
    cosine = jnp.cos(angles)[:, None, :]
    sine = jnp.sin(angles)[:, None, :]
    first = values[..., :half_width]
    second = values[..., half_width:]
    return jnp.concatenate(
        [first * cosine - second * sine, second * cosine + first * sine], axis=-1
    )


def on_device(
    tokens,
    norm_gain,
    w_query,
    key_weight,
    value_weight,
    query_gain,
    key_gain,
    w_out,
    doc_ids,
    sentinel,
    tile_reach,
):
    whole = lax.all_gather(tokens, "head", axis=1, tiled=True)
    row_count = whole.shape[0]
    normalized_rows = rms_norm(whole.astype(jnp.float32), norm_gain).astype(jnp.bfloat16)
    query_cols = w_query.shape[1]
    key_cols = key_weight.shape[1]
    portions = (
        lax.all_gather(w_query, "tok", axis=0, tiled=True),
        lax.all_gather(key_weight, "tok", axis=0, tiled=True),
        lax.all_gather(value_weight, "tok", axis=0, tiled=True),
    )
    proj_query, proj_key, proj_value = tuple(
        (
            jnp.dot(normalized_rows, portion, preferred_element_type=jnp.float32)
            for portion in portions
        )
    )
    base_row = lax.axis_index("tok") * row_count
    positions = (base_row + jnp.arange(row_count, dtype=jnp.int32)).astype(jnp.float32)
    local_heads = query_cols // HEAD_SIZE
    local_kv = key_cols // HEAD_SIZE
    head_groups = local_heads // local_kv
    query_matrix = rotate(
        rms_norm(proj_query.reshape(row_count, local_heads, HEAD_SIZE), query_gain), positions
    )
    query_matrix = query_matrix.astype(jnp.bfloat16).reshape(
        row_count, local_kv, head_groups, HEAD_SIZE
    )
    keys_own = rotate(
        rms_norm(proj_key.reshape(row_count, local_kv, HEAD_SIZE), key_gain), positions
    ).astype(jnp.bfloat16)
    values_own = proj_value.astype(jnp.bfloat16).reshape(row_count, local_kv, HEAD_SIZE)
    tags_own = jnp.where(sentinel == 1, 0, doc_ids + 1).astype(jnp.bfloat16)
    blocks = REACH_DEVS + 1

    def pass_along(step_index, state):
        current, key_store, value_store, tag_store = state
        current = passed_along((current[0], current[1], current[2]), "tok", 1)
        slot = REACH_DEVS - 1 - step_index
        key_store = lax.dynamic_update_index_in_dim(key_store, current[0], slot, 0)
        value_store = lax.dynamic_update_index_in_dim(value_store, current[1], slot, 0)
        tag_store = lax.dynamic_update_index_in_dim(tag_store, current[2], slot, 0)
        return (current, key_store, value_store, tag_store)

    key_store = (
        jnp.zeros((blocks, row_count, local_kv, HEAD_SIZE), jnp.bfloat16)
        .at[REACH_DEVS]
        .set(keys_own)
    )
    value_store = (
        jnp.zeros((blocks, row_count, local_kv, HEAD_SIZE), jnp.bfloat16)
        .at[REACH_DEVS]
        .set(values_own)
    )
    tag_store = jnp.zeros((blocks, row_count), jnp.bfloat16).at[REACH_DEVS].set(tags_own)
    state = lax.fori_loop(
        0,
        REACH_DEVS,
        pass_along,
        ((keys_own, values_own, tags_own), key_store, value_store, tag_store),
    )
    key_store, value_store, tag_store = (state[1], state[2], state[3])
    factor_scale = 1.0 / math.sqrt(HEAD_SIZE)
    outputs = []
    for tile_index in range(row_count // TILE_TOKENS):
        query_tile = query_matrix[tile_index * TILE_TOKENS : (tile_index + 1) * TILE_TOKENS]
        query_pos = base_row + tile_index * TILE_TOKENS + jnp.arange(TILE_TOKENS, dtype=jnp.int32)
        query_docs = doc_ids[tile_index * TILE_TOKENS : (tile_index + 1) * TILE_TOKENS] + 1
        lowest = base_row // TILE_TOKENS + tile_index - tile_reach[tile_index]

        def update(
            block,
            state,
            query_tile=query_tile,
            query_pos=query_pos,
            query_docs=query_docs,
            lowest=lowest,
        ):
            key_block = key_store[block]
            value_block = value_store[block]
            tag_block = tag_store[block].astype(jnp.int32)
            key_pos = (
                base_row + (block - REACH_DEVS) * row_count + jnp.arange(row_count, dtype=jnp.int32)
            )
            same_doc = (tag_block[None, :] == query_docs[:, None]) | (
                key_pos[None, :] == query_pos[:, None]
            )
            visible = (
                same_doc
                & (key_pos[None, :] <= query_pos[:, None])
                & (jnp.floor_divide(key_pos, TILE_TOKENS)[None, :] >= lowest)
            )

            def compute(inner):
                peak_run, weight_sum, accum_out = inner
                scores = (
                    jnp.einsum(
                        "qcgd,kcd->cgqk", query_tile, key_block, preferred_element_type=jnp.float32
                    )
                    * factor_scale
                )
                scores = jnp.where(visible, scores, -jnp.inf)
                peak_new = jnp.maximum(peak_run, jnp.max(scores, axis=-1))
                shrink = jnp.exp(peak_run - peak_new)
                weights = jnp.exp(scores - peak_new[..., None])
                weight_sum = weight_sum * shrink + jnp.sum(weights, axis=-1)
                mixed = jnp.einsum(
                    "cgqk,kcd->cgqd",
                    weights.astype(jnp.bfloat16),
                    value_block,
                    preferred_element_type=jnp.float32,
                )
                return (peak_new, weight_sum, accum_out * shrink[..., None] + mixed)

            return lax.cond(jnp.any(visible), compute, lambda inner: inner, state)

        initial = (
            jnp.full((local_kv, head_groups, TILE_TOKENS), -1e30, jnp.float32),
            jnp.zeros((local_kv, head_groups, TILE_TOKENS), jnp.float32),
            jnp.zeros((local_kv, head_groups, TILE_TOKENS, HEAD_SIZE), jnp.float32),
        )
        peak_run, weight_sum, accum_out = lax.fori_loop(0, blocks, update, initial)
        result = accum_out / weight_sum[..., None]
        outputs.append(
            jnp.transpose(result, (2, 0, 1, 3))
            .reshape(TILE_TOKENS, query_cols)
            .astype(jnp.bfloat16)
        )
    attended = jnp.concatenate(outputs, axis=0)
    partials = jnp.dot(
        attended,
        lax.all_gather(w_out, "tok", axis=1, tiled=True),
        preferred_element_type=jnp.float32,
    )
    return lax.psum_scatter(partials.astype(jnp.bfloat16), "head", scatter_dimension=1, tiled=True)


CHUNK = 256
MESH_IDS = pl.DeviceIdType.MESH
MASKED = -1e30


def send(source, target, send_sem, recv_sem, device):
    return pltpu.make_async_remote_copy(
        src_ref=source,
        dst_ref=target,
        send_sem=send_sem,
        recv_sem=recv_sem,
        device_id={"tok": device},
        device_id_type=MESH_IDS,
    )


def head_norm_rotate(values, gain, cosine, sine):
    mean_square = jnp.mean(values * values, axis=-1, keepdims=True)
    normed = values * lax.rsqrt(mean_square + EPSILON) * gain
    return normed * cosine + pltpu.roll(normed, HEAD_SIZE // 2, 1) * sine


def project_kernel(
    members,
    groups,
    reach_rows,
    normed_ref,
    pack_ref,
    out_pack_ref,
    cos_ref,
    sin_ref,
    query_gain_ref,
    key_gain_ref,
    facts_ref,
    query_ref,
    window_ref,
    out_block_ref,
    facts_window_ref,
    rows_all,
    weights_all,
    kv_own,
    own_sems,
    pack_send,
    pack_recv,
    out_send,
    out_recv,
    row_send,
    row_recv,
    block_send,
    block_recv,
    kv_send,
    kv_recv,
    fact_send,
    fact_recv,
    past_send,
    past_recv,
):
    me = lax.axis_index("tok")
    g = lax.rem(me, members)
    t = lax.div(me, members)
    y = lax.rem(t, 2)
    z = lax.div(t, 2)
    depth_z = groups // 2
    base = t * members
    side = me + members * (1 - 2 * y)
    below, above = me - 2 * members, me + 2 * members
    row_count = normed_ref.shape[0]
    group_rows = members * row_count
    back = -(-reach_rows // group_rows)
    window_rows = window_ref.shape[0]

    barrier = pltpu.get_barrier_semaphore()
    for step in range(1, members):
        other = base + lax.rem(g + step, members)
        pl.semaphore_signal(barrier, inc=1, device_id={"tok": other}, device_id_type=MESH_IDS)
    span = max(back, 2)
    peers = members - 1
    for delta in [*range(-span, 0), *range(1, span + 1)]:
        present = (t + delta >= 0) & (t + delta < groups)
        peers = peers + present.astype(jnp.int32)

        @pl.when(present)
        def _(delta=delta):
            pl.semaphore_signal(
                barrier, inc=1, device_id={"tok": me + delta * members}, device_id_type=MESH_IDS
            )

    pl.semaphore_wait(barrier, peers)

    own = [
        pltpu.make_async_copy(pack_ref.at[g], weights_all.at[t, g], own_sems.at[0]),
        pltpu.make_async_copy(out_pack_ref.at[g], out_block_ref.at[g], own_sems.at[1]),
        pltpu.make_async_copy(normed_ref, rows_all.at[g], own_sems.at[2]),
        pltpu.make_async_copy(facts_ref, facts_window_ref.at[back, g], own_sems.at[3]),
    ]

    def fact_copy(step):
        j = lax.rem(g + step, members)
        return send(
            facts_ref, facts_window_ref.at[back, g], fact_send.at[step], fact_recv.at[step], base + j
        )

    def past_copy(distance):
        return send(
            facts_window_ref.at[back],
            facts_window_ref.at[back - distance],
            past_send.at[distance - 1],
            past_recv.at[distance - 1],
            me + distance * members,
        )


    def pack_copy(step):
        j = lax.rem(g + step, members)
        return send(
            pack_ref.at[j], weights_all.at[t, g], pack_send.at[step], pack_recv.at[step], base + j
        )

    def out_copy(step):
        j = lax.rem(g + step, members)
        return send(
            out_pack_ref.at[j], out_block_ref.at[g], out_send.at[step], out_recv.at[step], base + j
        )

    partner = base + g + 1 - 2 * lax.rem(g, 2)
    across_g = lax.rem(g + 2, members)
    across = base + across_g
    row_copies = [
        send(normed_ref, rows_all.at[g], row_send.at[0], row_recv.at[0], partner),
        send(normed_ref, rows_all.at[g], row_send.at[1], row_recv.at[1], across),
        send(rows_all.at[across_g], rows_all.at[across_g], row_send.at[2], row_recv.at[2], partner),
    ]
    for copy in own:
        copy.start()
    for step in range(1, members):
        fact_copy(step).start()
        pack_copy(step).start()
    row_copies[1].start()
    row_copies[0].start()
    for step in range(1, members):
        pack_copy(step).wait_recv()
    own[0].wait()

    def block_copy(block, way, device):
        return send(
            weights_all.at[block],
            weights_all.at[block],
            block_send.at[block, way],
            block_recv.at[block],
            device,
        )

    def forward(block, up, down):
        if up:

            @pl.when(z < depth_z - 1)
            def _():
                block_copy(block, 0, above).start()

        if down:

            @pl.when(z > 0)
            def _():
                block_copy(block, 1, below).start()

        block_copy(block, 2, side).start()

    def forward_done(block, up, down):
        if up:

            @pl.when(z < depth_z - 1)
            def _():
                block_copy(block, 0, above).wait_send()

        if down:

            @pl.when(z > 0)
            def _():
                block_copy(block, 1, below).wait_send()

        block_copy(block, 2, side).wait_send()

    forward(t, True, True)
    for step in range(1, members):
        out_copy(step).start()
        fact_copy(step).wait_recv()
    own[3].wait()
    for distance in range(1, back + 1):

        @pl.when(t + distance < groups)
        def _(distance=distance):
            past_copy(distance).start()

        @pl.when(t < distance)
        def _(distance=distance):
            facts_window_ref[back - distance] = jnp.full(
                facts_window_ref.shape[1:], -1, jnp.int32
            )

    row_copies[1].wait_recv()
    row_copies[2].start()
    for k in range(1, depth_z):

        @pl.when(z >= k)
        def _(k=k):
            block_copy(t - 2 * k, 0, above).wait_recv()
            forward(t - 2 * k, True, False)

        @pl.when(z + k < depth_z)
        def _(k=k):
            block_copy(t + 2 * k, 1, below).wait_recv()
            forward(t + 2 * k, False, True)

    row_copies[0].wait_recv()
    row_copies[2].wait_recv()
    own[1].wait()
    own[2].wait()
    for k in range(depth_z):
        block_copy(2 * k + 1 - y, 2, side).wait_recv()

    model = weights_all.shape[1] * weights_all.shape[2] * groups
    columns = weights_all.shape[3]
    query_cols = columns - 2 * HEAD_SIZE
    share = row_count
    width_k = model // groups

    def project(member, start, size):
        def add(block, total):
            piece = rows_all[member, :, pl.ds(pl.multiple_of(block * width_k, width_k), width_k)]
            weight = weights_all[block, :, :, pl.ds(start, size)].reshape(width_k, size)
            return total + jnp.dot(piece, weight, preferred_element_type=jnp.float32)

        total = jnp.zeros((row_count, size), jnp.float32)
        return lax.fori_loop(0, groups, add, total, unroll=True)

    @pl.loop(0, members)
    def _(member):
        rows = pl.ds(pl.multiple_of(member * share, share), share)
        both = project(member, query_cols, 2 * HEAD_SIZE)
        key = head_norm_rotate(
            both[:, :HEAD_SIZE], key_gain_ref[...], cos_ref[rows, :], sin_ref[rows, :]
        )
        kv_own[rows, :HEAD_SIZE] = key.astype(jnp.bfloat16)
        kv_own[rows, HEAD_SIZE:] = both[:, HEAD_SIZE:].astype(jnp.bfloat16)

    def slot(distance):
        full = window_rows - (distance + 1) * group_rows
        low = window_rows - group_rows - reach_rows
        skip = max(0, low - full)
        return skip, full + skip

    def slot_ref(distance, skipped=0):
        skip, start = slot(distance)
        drop = max(skipped - skip, 0)
        return window_ref.at[pl.ds(start + drop, group_rows - skip - drop)]

    far_skip = slot(4)[0]

    def kv_copy(source, distance, way, device):
        return send(
            source, slot_ref(distance), kv_send.at[way], kv_recv.at[distance - 1], device
        )

    own_up = kv_copy(kv_own, 2, 0, above)
    own_side = kv_copy(kv_own, 1, 1, side)
    second_side_low = kv_copy(slot_ref(2), 3, 2, side)
    second_side_high = kv_copy(slot_ref(2), 1, 2, side)
    second_up = kv_copy(slot_ref(2, far_skip), 4, 3, above)
    first_up = kv_copy(slot_ref(1), 3, 4, above)
    has_above = z < depth_z - 1

    def kv_wait(distance):
        kv_copy(slot_ref(distance), distance, 0, side).wait_recv()

    @pl.when(has_above)
    def _():
        own_up.start()

    @pl.when(y == 0)
    def _():
        own_side.start()

    for distance in range(back, 0, -1):

        @pl.when(t < distance)
        def _(distance=distance):
            skip, start = slot(distance)
            window_ref[start : start + group_rows - skip, :] = jnp.zeros(
                (group_rows - skip, 2 * HEAD_SIZE), jnp.bfloat16
            )

    pad = window_rows - group_rows - reach_rows
    window_ref[:pad, :] = jnp.zeros((pad, 2 * HEAD_SIZE), jnp.bfloat16)

    pair = 2 * HEAD_SIZE

    def project_queries(first, last):
        @pl.loop(first, last)
        def _(member):
            rows = pl.ds(pl.multiple_of(member * share, share), share)
            place = pl.multiple_of(window_rows - group_rows + member * share, 128)
            window_ref[pl.ds(place, share), :] = kv_own[rows, :]

            @pl.loop(0, query_cols // pair)
            def _(h):
                both = project(member, pl.multiple_of(h * pair, pair), pair)
                for half in range(2):
                    head = head_norm_rotate(
                        both[:, half * HEAD_SIZE : (half + 1) * HEAD_SIZE],
                        query_gain_ref[...],
                        cos_ref[rows, :],
                        sin_ref[rows, :],
                    )
                    query_ref[2 * h + half, rows, :] = head.astype(jnp.bfloat16)

    project_queries(0, members // 2)

    @pl.when(z >= 1)
    def _():
        kv_wait(2)

        @pl.when(has_above)
        def _():
            second_up.start()

        @pl.when(y == 0)
        def _():
            second_side_low.start()

        @pl.when(y == 1)
        def _():
            second_side_high.start()

    project_queries(members // 2, members)

    @pl.when((y == 0) & (z >= 1))
    def _():
        kv_wait(1)

        @pl.when(has_above)
        def _():
            first_up.start()

    @pl.when(y == 1)
    def _():
        kv_wait(1)

    for distance in (3, 4):

        @pl.when(t >= distance)
        def _(distance=distance):
            kv_wait(distance)

    @pl.when(has_above)
    def _():
        own_up.wait_send()

        @pl.when(z >= 1)
        def _():
            second_up.wait_send()

    @pl.when(y == 0)
    def _():
        own_side.wait_send()

    @pl.when(z >= 1)
    def _():
        @pl.when(y == 0)
        def _():
            second_side_low.wait_send()

            @pl.when(has_above)
            def _():
                first_up.wait_send()

        @pl.when(y == 1)
        def _():
            second_side_high.wait_send()

    for distance in range(1, back + 1):

        @pl.when(t >= distance)
        def _(distance=distance):
            past_copy(distance).wait_recv()

        @pl.when(t + distance < groups)
        def _(distance=distance):
            past_copy(distance).wait_send()

    for step in range(1, members):
        pack_copy(step).wait_send()
        fact_copy(step).wait_send()
        out_copy(step).wait()
    for copy in row_copies:
        copy.wait_send()
    forward_done(t, True, True)
    for k in range(1, depth_z):

        @pl.when(z >= k)
        def _(k=k):
            forward_done(t - 2 * k, True, False)

        @pl.when(z + k < depth_z)
        def _(k=k):
            forward_done(t + 2 * k, False, True)


def attention_kernel(counts, floors, query_ref, docs_ref, window_ref, tags_ref, out_ref, acc, peak, total):
    tile = pl.program_id(0)
    heads = query_ref.shape[0]
    window_rows = window_ref.shape[0]
    tiles = pl.num_programs(0)
    end = window_rows - (tiles - 1 - tile) * TILE_TOKENS
    factor = math.log2(math.e) / math.sqrt(HEAD_SIZE)
    query_at = end - TILE_TOKENS + lax.broadcasted_iota(jnp.int32, (CHUNK, TILE_TOKENS), 1)
    peak[...] = jnp.full_like(peak, MASKED)
    total[...] = jnp.zeros_like(total)
    acc[...] = jnp.zeros_like(acc)

    @pl.loop(0, counts[tile])
    def _(step):
        start = pl.multiple_of(end - (step + 1) * CHUNK, TILE_TOKENS)
        keys = window_ref[pl.ds(start, CHUNK), :HEAD_SIZE]
        values = window_ref[pl.ds(start, CHUNK), HEAD_SIZE:].T
        key_at = start + lax.broadcasted_iota(jnp.int32, (CHUNK, TILE_TOKENS), 0)
        tags = tags_ref[pl.ds(start, CHUNK), :]
        visible = (
            ((tags == docs_ref[...]) | (key_at == query_at))
            & (key_at <= query_at)
            & (key_at >= floors[tile])
        )
        bias = jnp.where(visible, 0.0, MASKED)
        bias = jnp.concatenate([bias, bias], axis=1)
        for pair in range(heads // 2):
            queries = query_ref[2 * pair : 2 * pair + 2].reshape(2 * TILE_TOKENS, HEAD_SIZE)
            scores = lax.dot_general(
                keys, queries, (((1,), (1,)), ((), ())), preferred_element_type=jnp.float32
            )
            scores = scores * factor + bias
            before = peak[pair]
            now = jnp.maximum(before, jnp.max(scores, axis=0, keepdims=True))
            shrink = jnp.exp2(before - now)
            weights = jnp.exp2(scores - now)
            total[pair] = total[pair] * shrink + jnp.sum(weights, axis=0, keepdims=True)
            acc[pair] = acc[pair] * shrink + jnp.dot(
                values, weights.astype(jnp.bfloat16), preferred_element_type=jnp.float32
            )
            peak[pair] = now

    for pair in range(heads // 2):
        mixed = (acc[pair] / total[pair]).T.astype(jnp.bfloat16)
        for half in range(2):
            columns = slice((2 * pair + half) * HEAD_SIZE, (2 * pair + half + 1) * HEAD_SIZE)
            out_ref[:, columns] = mixed[half * TILE_TOKENS : (half + 1) * TILE_TOKENS]


def output_kernel(
    members,
    groups,
    attended_ref,
    block_ref,
    out_ref,
    weights_all,
    sums,
    near_out,
    near_in,
    far_out,
    far_in,
    own_sem,
    block_send,
    block_recv,
    near_send,
    near_recv,
    far_send,
    far_recv,
):
    me = lax.axis_index("tok")
    g = lax.rem(me, members)
    t = lax.div(me, members)
    y = lax.rem(t, 2)
    z = lax.div(t, 2)
    depth_z = groups // 2
    base = me - g
    partner_g = g + 1 - 2 * lax.rem(g, 2)
    across_g = lax.rem(g + 2, members)
    diagonal_g = lax.rem(partner_g + 2, members)
    partner, across = base + partner_g, base + across_g
    side = me + members * (1 - 2 * y)
    below, above = me - 2 * members, me + 2 * members
    row_count = out_ref.shape[0]
    width = block_ref.shape[0]
    barrier = pltpu.get_barrier_semaphore()
    for other in (partner, across, side):
        pl.semaphore_signal(barrier, inc=1, device_id={"tok": other}, device_id_type=MESH_IDS)

    @pl.when(z > 0)
    def _():
        pl.semaphore_signal(barrier, inc=1, device_id={"tok": below}, device_id_type=MESH_IDS)

    @pl.when(z < depth_z - 1)
    def _():
        pl.semaphore_signal(barrier, inc=1, device_id={"tok": above}, device_id_type=MESH_IDS)

    own = pltpu.make_async_copy(block_ref, weights_all.at[t], own_sem)
    own.start()
    own.wait()
    pl.semaphore_wait(barrier, 3 + (z > 0).astype(jnp.int32) + (z < depth_z - 1).astype(jnp.int32))

    def block_copy(block, way, device):
        return send(
            weights_all.at[block],
            weights_all.at[block],
            block_send.at[block, way],
            block_recv.at[block],
            device,
        )

    near_z = jnp.minimum(z, depth_z - 1 - z)

    def plane(turn):
        step = lax.div(turn + 1, 2)
        both = z + step * (1 - 2 * lax.rem(turn, 2))
        rest = jnp.where(2 * z < depth_z - 1, turn, depth_z - 1 - turn)
        return jnp.where(turn <= 2 * near_z, both, rest)

    def block_at(turn):
        level = plane(lax.div(turn, 2))
        row = jnp.where(lax.rem(turn, 2) == 0, y, 1 - y)
        return level, 2 * level + row

    def partial(member, block):
        rows = pl.ds(pl.multiple_of(member * row_count, row_count), row_count)
        return lax.dot_general(
            attended_ref[rows, :],
            weights_all[block],
            (((1,), (1,)), ((), ())),
            preferred_element_type=jnp.float32,
        ).astype(jnp.bfloat16)

    def near(way, turn):
        return send(
            near_out.at[way, turn],
            near_in.at[way, turn],
            near_send.at[way, turn],
            near_recv.at[way, turn],
            partner,
        )

    def far(turn):
        return send(far_out.at[turn], far_in.at[turn], far_send.at[turn], far_recv.at[turn], across)

    @pl.loop(0, groups + 1)
    def _(turn):
        @pl.when(turn < groups)
        def _():
            level, block = block_at(turn)
            mine = lax.rem(turn, 2) == 0

            @pl.when(turn > 0)
            def _():
                block_copy(block, 2, side).wait_recv()

            @pl.when(mine & (level <= z) & (z < depth_z - 1))
            def _():
                block_copy(block, 0, above).start()

            @pl.when(mine & (level >= z) & (z > 0))
            def _():
                block_copy(block, 1, below).start()

            @pl.when(mine)
            def _():
                block_copy(block, 2, side).start()

            near_out[0, turn] = partial(diagonal_g, block)
            near(0, turn).start()
            near_out[1, turn] = partial(partner_g, block)
            near(1, turn).start()

        @pl.when(turn > 0)
        def _():
            past = turn - 1
            _, block = block_at(past)
            first = partial(across_g, block).astype(jnp.float32)
            near(0, past).wait_recv()
            far_out[past] = (first + near_in[0, past].astype(jnp.float32)).astype(jnp.bfloat16)
            far(past).start()
            second = partial(g, block).astype(jnp.float32)
            near(1, past).wait_recv()
            sums[past] = second + near_in[1, past].astype(jnp.float32)

    @pl.loop(0, groups)
    def _(turn):
        level, block = block_at(turn)
        mine = lax.rem(turn, 2) == 0
        far(turn).wait_recv()
        out_ref[:, pl.ds(pl.multiple_of(block * width, width), width)] = (
            sums[turn] + far_in[turn].astype(jnp.float32)
        ).astype(jnp.bfloat16)
        near(0, turn).wait_send()
        near(1, turn).wait_send()
        far(turn).wait_send()

        @pl.when(mine & (level <= z) & (z < depth_z - 1))
        def _():
            block_copy(block, 0, above).wait_send()

        @pl.when(mine & (level >= z) & (z > 0))
        def _():
            block_copy(block, 1, below).wait_send()

        @pl.when(mine)
        def _():
            block_copy(block, 2, side).wait_send()


VMEM_BYTES = 60 << 20


def in_vmem(count):
    return [pl.BlockSpec(memory_space=pltpu.VMEM)] * count


def grouped(
    tokens,
    norm_gain,
    w_query,
    key_weight,
    value_weight,
    query_gain,
    key_gain,
    w_out,
    doc_ids,
    sentinel,
    tile_reach,
):
    row_count = tokens.shape[0]
    depth = w_query.shape[0]
    members = key_weight.shape[1] // HEAD_SIZE
    devices = lax.axis_size("tok")
    groups = devices // members
    group_rows = members * row_count
    reach_rows = REACH_DEVS * row_count
    pad = CHUNK - TILE_TOKENS
    window_rows = pad + reach_rows + group_rows
    query_cols = w_query.shape[1] // members
    heads = query_cols // HEAD_SIZE
    model = tokens.shape[1]
    group = lax.axis_index("tok") // members
    base_row = group * group_rows

    lanes = HEAD_SIZE
    rows_each = row_count // lanes
    facts = jnp.concatenate(
        [
            doc_ids,
            sentinel,
            jnp.pad(tile_reach, (0, (8 - 2 * rows_each) * lanes - tile_reach.shape[0])),
        ]
    ).reshape(8, lanes)

    normed = rms_norm(tokens.astype(jnp.float32), norm_gain).astype(jnp.bfloat16)
    pack = jnp.concatenate(
        [
            w_query.reshape(depth, members, query_cols),
            key_weight.reshape(depth, members, HEAD_SIZE),
            value_weight.reshape(depth, members, HEAD_SIZE),
        ],
        axis=2,
    ).transpose(1, 0, 2)
    out_depth = w_out.shape[1]
    out_pack = w_out.T.reshape(out_depth, members, query_cols).transpose(1, 0, 2)
    positions = (base_row + jnp.arange(group_rows, dtype=jnp.int32)).astype(jnp.float32)
    half_width = HEAD_SIZE // 2
    freqs = THETA ** (-2.0 * jnp.arange(half_width, dtype=jnp.float32) / HEAD_SIZE)
    angles = positions[:, None] * freqs[None, :]
    cosine, sine = jnp.cos(angles), jnp.sin(angles)
    cosine = jnp.concatenate([cosine, cosine], axis=1)
    sine = jnp.concatenate([-sine, sine], axis=1)
    columns = query_cols + 2 * HEAD_SIZE
    back = -(-reach_rows // group_rows)
    dma = pltpu.SemaphoreType.DMA
    queries, window, out_block, facts_window = pl.pallas_call(
        functools.partial(project_kernel, members, groups, reach_rows),
        out_shape=(
            jax.ShapeDtypeStruct((heads, group_rows, HEAD_SIZE), jnp.bfloat16),
            jax.ShapeDtypeStruct((window_rows, 2 * HEAD_SIZE), jnp.bfloat16),
            jax.ShapeDtypeStruct((members, out_depth, query_cols), jnp.bfloat16),
            jax.ShapeDtypeStruct((back + 1, members, 8, lanes), jnp.int32),
        ),
        in_specs=in_vmem(8),
        out_specs=tuple(in_vmem(4)),
        scratch_shapes=[
            pltpu.VMEM((members, row_count, model), jnp.bfloat16),
            pltpu.VMEM((groups, members, depth, columns), jnp.bfloat16),
            pltpu.VMEM((group_rows, 2 * HEAD_SIZE), jnp.bfloat16),
            dma((4,)),
            dma((members,)),
            dma((members,)),
            dma((members,)),
            dma((members,)),
            dma((3,)),
            dma((3,)),
            dma((groups, 3)),
            dma((groups,)),
            dma((5,)),
            dma((back,)),
            dma((members,)),
            dma((members,)),
            dma((back,)),
            dma((back,)),
        ],
        compiler_params=pltpu.CompilerParams(
            collective_id=0, has_side_effects=True, vmem_limit_bytes=VMEM_BYTES
        ),
        name="project",
    )(normed, pack, out_pack, cosine, sine, query_gain[None, :], key_gain[None, :], facts)

    docs_all = facts_window[:, :, :rows_each].reshape(-1)[-window_rows:]
    sentinel_all = facts_window[:, :, rows_each : 2 * rows_each].reshape(-1)[-window_rows:]
    tags_window = jnp.where(sentinel_all == 1, 0, docs_all + 1)
    tags_window = jnp.broadcast_to(tags_window[:, None], (window_rows, TILE_TOKENS))
    tiles = group_rows // TILE_TOKENS
    query_docs = docs_all[-group_rows:]
    reach = facts_window[back, :, 2 * rows_each, : tile_reach.shape[0]].reshape(-1)
    first_row = window_rows - group_rows
    tile_start = first_row + jnp.arange(tiles, dtype=jnp.int32) * TILE_TOKENS
    first_doc = query_docs[::TILE_TOKENS]
    doc_start = jnp.sum((docs_all[None, :] < first_doc[:, None]).astype(jnp.int32), axis=1)
    floors = tile_start - reach * TILE_TOKENS
    lowest = jnp.maximum(floors, doc_start // TILE_TOKENS * TILE_TOKENS)
    counts = (tile_start + TILE_TOKENS - lowest + CHUNK - 1) // CHUNK

    attended = pl.pallas_call(
        attention_kernel,
        out_shape=jax.ShapeDtypeStruct((group_rows, query_cols), jnp.bfloat16),
        grid_spec=pltpu.PrefetchScalarGridSpec(
            num_scalar_prefetch=2,
            grid=(tiles,),
            in_specs=[
                pl.BlockSpec((heads, TILE_TOKENS, HEAD_SIZE), lambda i, *_: (0, i, 0)),
                pl.BlockSpec((1, TILE_TOKENS), lambda i, *_: (0, i)),
                pl.BlockSpec((window_rows, 2 * HEAD_SIZE), lambda i, *_: (0, 0)),
                pl.BlockSpec((window_rows, TILE_TOKENS), lambda i, *_: (0, 0)),
            ],
            out_specs=pl.BlockSpec((TILE_TOKENS, query_cols), lambda i, *_: (i, 0)),
            scratch_shapes=[
                pltpu.VMEM((heads // 2, HEAD_SIZE, 2 * TILE_TOKENS), jnp.float32),
                pltpu.VMEM((heads // 2, 1, 2 * TILE_TOKENS), jnp.float32),
                pltpu.VMEM((heads // 2, 1, 2 * TILE_TOKENS), jnp.float32),
            ],
        ),
        compiler_params=pltpu.CompilerParams(vmem_limit_bytes=VMEM_BYTES),
        cost_estimate=pl.CostEstimate(
            flops=2 * group_rows * window_rows * query_cols,
            bytes_accessed=window_rows * 4 * HEAD_SIZE + 4 * group_rows * query_cols,
            transcendentals=group_rows * window_rows * heads // 2,
        ),
        name="attend",
    )(counts, floors, queries, query_docs[None, :] + 1, window, tags_window)

    width = members * out_depth
    return pl.pallas_call(
        functools.partial(output_kernel, members, groups),
        out_shape=jax.ShapeDtypeStruct((row_count, model), jnp.bfloat16),
        in_specs=in_vmem(2),
        out_specs=in_vmem(1)[0],
        scratch_shapes=[
            pltpu.VMEM((groups, width, query_cols), jnp.bfloat16),
            pltpu.VMEM((groups, row_count, width), jnp.float32),
            pltpu.VMEM((2, groups, row_count, width), jnp.bfloat16),
            pltpu.VMEM((2, groups, row_count, width), jnp.bfloat16),
            pltpu.VMEM((groups, row_count, width), jnp.bfloat16),
            pltpu.VMEM((groups, row_count, width), jnp.bfloat16),
            dma,
            dma((groups, 3)),
            dma((groups,)),
            dma((2, groups)),
            dma((2, groups)),
            dma((groups,)),
            dma((groups,)),
        ],
        compiler_params=pltpu.CompilerParams(
            collective_id=1, has_side_effects=True, vmem_limit_bytes=VMEM_BYTES
        ),
        name="output",
    )(attended, out_block.reshape(width, query_cols))


def chosen(*arguments):
    members = arguments[3].shape[1] // HEAD_SIZE
    devices = lax.axis_size("tok")
    near_enough = 3 * members < REACH_DEVS <= 4 * members
    if lax.axis_size("head") == 1 and members == 4 and near_enough and devices % 8 == 0:
        return grouped(*arguments)
    return on_device(*arguments)


def solution(mesh):
    return jax.shard_map(
        chosen,
        mesh=mesh,
        in_specs=(
            P("tok", "head"),
            P(),
            P("tok", "head"),
            P("tok", "head"),
            P("tok", "head"),
            P(),
            P(),
            P("head", "tok"),
            P("tok"),
            P("tok"),
            P("tok"),
        ),
        out_specs=P("tok", "head"),
        check_vma=False,
    )
```
